32 devices in a mesh: dp: 8 (over z, y), head: 4 (over x, core).
Axes of the slice: x: 2, y: 2, z: 4, core: 2. Of those that a mesh axis runs over, the one named last changes fastest.
Arguments:
- features: bfloat16 [16, 64, 1024], P('dp', 'head'), may hold values from -6 to 6
- style_code: bfloat16 [16, 512], P('dp'), may hold values from -6 to 6
- labels: int32 [16], P('dp'), may hold values from 0 to 1023
- counts: int32 [8], P('dp'), may hold values from 1 to 2, as said below
- context: bfloat16 [16, 16, 1024], P('dp'), may hold values from -6 to 6
- noise_map: bfloat16 [16, 256], P('dp'), may hold values from -6 to 6
- w_select: bfloat16 [512, 8], P('dp'), may hold values from -0.5 to 0.5
- w_mod: bfloat16 [512, 1024], P('dp'), may hold values from -0.119628906 to 0.119628906
- kernel_bank: bfloat16 [8, 9, 1024, 1024], P(None, None, 'dp', 'head'), may hold values from -0.0625 to 0.0625
- conv_vecs: bfloat16 [2, 1024], P(None, 'dp'), may hold values from -3.5 to 3.5
- class_table: bfloat16 [1024, 1024], P('dp'), may hold values from -6 to 6
- w_qkv: bfloat16 [2, 1024, 1024], P(None, 'dp', 'head'), may hold values from -0.09375 to 0.09375
- w_attn_out: bfloat16 [1024, 1024], P('head', 'dp'), may hold values from -1 to 1
- w_cross_q: bfloat16 [1024, 1024], P('dp', 'head'), may hold values from -0.0625 to 0.0625
- w_cross_kv: bfloat16 [2, 1024, 1024], P(None, 'dp', 'head'), may hold values from -0.1875 to 0.1875
- w_cross_out: bfloat16 [1024, 1024], P('head', 'dp'), may hold values from -0.375 to 0.375
- w_mlp_in: bfloat16 [1024, 4096], P('dp', 'head'), may hold values from -0.1875 to 0.1875
- w_mlp_out: bfloat16 [4096, 1024], P('head', 'dp'), may hold values from -0.125 to 0.125
- w_rgb: bfloat16 [3, 1024], P(None, 'dp'), may hold values from -0.1875 to 0.1875
- cot_feat: bfloat16 [16, 256, 1024], P('dp', 'head'), may hold values from -6 to 6
- cot_rgb: bfloat16 [16, 3, 256], P('dp', None, 'head'), may hold values from -6 to 6
Outputs:
- features_out: bfloat16 [16, 256, 1024], P('dp', 'head')
- rgb_out: bfloat16 [16, 3, 256], P('dp', None, 'head')
- grad_input: float32 [16, 64, 1024], P('dp', 'head')
- grad_select: float32 [512, 8], P('dp')
- grad_mod: float32 [512, 1024], P('dp')
- grad_bank: float32 [8, 9, 1024, 1024], P(None, None, 'dp', 'head')
- grad_vecs: float32 [2, 1024], P(None, 'dp')
- grad_table: float32 [1024, 1024], P('dp')
- grad_qkv: float32 [2, 1024, 1024], P(None, 'dp', 'head')
- grad_attn_out: float32 [1024, 1024], P('head', 'dp')
- grad_cross_q: float32 [1024, 1024], P('dp', 'head')
- grad_cross_kv: float32 [2, 1024, 1024], P(None, 'dp', 'head')
- grad_cross_out: float32 [1024, 1024], P('head', 'dp')
- grad_mlp_in: float32 [1024, 4096], P('dp', 'head')
- grad_mlp_out: float32 [4096, 1024], P('head', 'dp')
- grad_rgb: float32 [3, 1024], P(None, 'dp')
The draws below stay inside these ranges and needn't reach their ends.
Inputs may be any that keep to these rules, and one draw needn't show every extreme that they name: `counts`: each entry is the number of live slots of one index of dp; slots below it are live and the rest empty. At least one entry equals 2 in every draw.
All inputs are finite; a program needn't handle non-finite values.
Results may differ from the reference program's by a relative error of at most 0.03.
The reference program's roundings to bfloat16 on the way count: a program that leaves them out, or rounds other values in their place, can miss the bound.
Values may be sent and summed in bfloat16 or wider, within the bound.
No kernel may reach another device: no remote copies, remote signals or barrier semaphores. Data moves between devices by JAX's collectives and lax.ppermute only.
A program may use at most 512 MiB of HBM per device.

```python
import jax
import jax.numpy as jnp
from jax import lax

D = 1024
STYLE = 512
HEADS = 16
DH = 64
KB = 8
FF = 4096
NCLASS = 1024
CT = 16
SLOTS = 2
RES = 16
PIX = 256
PIX_IN = 64
GROUPS = 8
BS = 16


def draw_counts(key, part):
    base = jax.random.randint(jax.random.fold_in(key, 11), (GROUPS,), 1, SLOTS + 1)
    chosen = jax.random.randint(jax.random.fold_in(key, 12), (), 0, GROUPS)
    return jnp.where(jnp.arange(GROUPS) == chosen, SLOTS, base).astype(jnp.int32)


def draw_conv_vecs(key, part):
    strength = jnp.clip(0.5 * jax.random.normal(jax.random.fold_in(key, 21), (D,), jnp.float32), -1.5, 1.5)
    magnitude = jax.random.uniform(jax.random.fold_in(key, 22), (D,), jnp.float32, 2.5, 3.5)
    positive = jax.random.bernoulli(jax.random.fold_in(key, 23), 0.5, (D,))
    bias = jnp.where(positive, magnitude, -magnitude)
    return jnp.stack((strength, bias), axis=0).astype(jnp.bfloat16)


def set_ends(drawn, key, smallest, top_value):
    extent = drawn.shape
    spot = [jax.random.randint(jax.random.fold_in(key, axis), (), 0, extent[axis]) for axis in range(len(extent))]
    drawn = drawn.at[tuple(spot)].set(smallest)
    longest = extent.index(max(extent))
    spot[longest] = (spot[longest] + 1) % extent[longest]
    return drawn.at[tuple(spot)].set(top_value)


def block_scale(stream_key, shape, split, least, top_value):
    factor_of, own = 1.0, jax.random.fold_in(stream_key, 6)
    for axis_at, parts in split:
        steps = jnp.exp(jax.random.uniform(jax.random.fold_in(own, axis_at), (parts,), jnp.float32, least / len(split), top_value / len(split)))
        factor_of = factor_of * jnp.repeat(steps, shape[axis_at] // parts).reshape([-1 if axis == axis_at else 1 for axis in range(len(shape))])
    return factor_of


def normal_values(stream_key, extent, width, bound, pieces=(), held_as=jnp.bfloat16):
    drawn = jax.random.normal(stream_key, extent, jnp.float32) * width
    if len(pieces) > 0:
        drawn = block_scale(stream_key, extent, pieces, -0.22, 0.18) * drawn
    return jnp.clip(drawn, min=-bound, max=bound).astype(held_as)


def setup_inputs(seed: int = 0) -> dict:
    arg_keys = jax.random.split(jax.random.key(seed), 22)
    return {
        "features": normal_values(arg_keys[0], (BS, PIX_IN, D), 1.0, 6.0, ((0, 8), (1, 4))),
        "style_code": normal_values(arg_keys[1], (BS, STYLE), 1.0, 6.0, ((0, 8),)),
        "labels": set_ends(jax.random.randint(arg_keys[2], (BS,), 0, NCLASS), jax.random.fold_in(arg_keys[2], 1), 0, NCLASS - 1).astype(jnp.int32),
        "counts": draw_counts(jax.random.fold_in(arg_keys[21], 71), 0),
        "context": normal_values(arg_keys[4], (BS, CT, D), 1.0, 6.0, ((0, 8),)),
        "noise_map": normal_values(arg_keys[5], (BS, PIX), 1.0, 6.0, ((0, 8),)),
        "w_select": normal_values(arg_keys[6], (STYLE, KB), 0.09, 0.5, ((0, 8),)),
        "w_mod": normal_values(arg_keys[7], (STYLE, D), 0.02, 0.119628906, ((0, 8),)),
        "kernel_bank": normal_values(arg_keys[8], (KB, 9, D, D), (9 * D) ** -0.5, 0.0625, ((2, 8), (3, 4))),
        "conv_vecs": draw_conv_vecs(jax.random.fold_in(arg_keys[21], 71), 0),
        "class_table": normal_values(arg_keys[10], (NCLASS, D), 1.0, 6.0, ((0, 8),)),
        "w_qkv": normal_values(arg_keys[11], (2, D, D), (4 * D) ** -0.5, 0.09375, ((1, 8), (2, 4))),
        "w_attn_out": normal_values(arg_keys[12], (D, D), (D // 32) ** -0.5, 1.0, ((0, 4), (1, 8))),
        "w_cross_q": normal_values(arg_keys[13], (D, D), (9 * D) ** -0.5, 0.0625, ((0, 8), (1, 4))),
        "w_cross_kv": normal_values(arg_keys[14], (2, D, D), D ** -0.5, 0.1875, ((1, 8), (2, 4))),
        "w_cross_out": normal_values(arg_keys[15], (D, D), (D // 4) ** -0.5, 0.375, ((0, 4), (1, 8))),
        "w_mlp_in": normal_values(arg_keys[16], (D, FF), D ** -0.5, 0.1875, ((0, 8), (1, 4))),
        "w_mlp_out": normal_values(arg_keys[17], (FF, D), (FF // 2) ** -0.5, 0.125, ((0, 4), (1, 8))),
        "w_rgb": normal_values(arg_keys[18], (3, D), D ** -0.5, 0.1875, ((1, 8),)),
        "cot_feat": normal_values(arg_keys[19], (BS, PIX, D), 1.0, 6.0, ((0, 8), (1, 4))),
        "cot_rgb": normal_values(arg_keys[20], (BS, 3, PIX), 1.0, 6.0, ((0, 8), (2, 4))),
    }


@jax.custom_vjp
def low(v):
    return lax.optimization_barrier(v.astype(jnp.bfloat16)).astype(jnp.float32)

@jax.custom_vjp
def low_back(v):
    return v

def low_keep(v):
    return (low(v), None)

def low_pass(kept, grad):
    return (grad,)

def back_keep(v):
    return (v, None)

def back_low(kept, grad):
    return (low(grad),)
low.defvjp(low_keep, low_pass)
low_back.defvjp(back_keep, back_low)
HIGH = lax.Precision.HIGHEST
ROOT_TWO = 1.4142135623730951
SLOPE = 0.2
DEMOD_EPS = 1e-08

def leaky_relu(value):
    return jnp.where(value > 0, value, SLOPE * value) * ROOT_TWO

def block_forward(weights, block):
    w_select, w_mod, kernel_bank, conv_vecs, class_table, w_qkv, w_attn_out, w_cross_q, w_cross_kv, w_cross_out, w_mlp_in, w_mlp_out, w_rgb = weights
    features, style_code, labels, context, noise_map = block
    score_scale = DH ** (-0.5)
    logits = jnp.dot(style_code, w_select, precision=HIGH)
    mixing = low(jax.nn.softmax(logits, axis=-1))
    modulate = 1.0 + jnp.dot(style_code, w_mod, precision=HIGH)
    kernels = low_back(low(jnp.einsum('sk,ktio->stio', mixing, kernel_bank, precision=HIGH)))
    square_sum = jnp.einsum('stio,si->so', kernels * kernels, modulate * modulate, precision=HIGH)
    demodulate = lax.rsqrt(square_sum + DEMOD_EPS)
    half_side = RES // 2
    grid_in = features.reshape(SLOTS, half_side, half_side, D)
    upsampled = jnp.repeat(jnp.repeat(grid_in, 2, axis=1), 2, axis=2)
    modulated = low(upsampled * modulate[:, None, None, :])
    padded = jnp.pad(modulated, ((0, 0), (1, 1), (1, 1), (0, 0)))
    conv_sum = jnp.zeros((SLOTS, RES, RES, D), jnp.float32)
    for tap_index in range(9):
        row_off = tap_index // 3
        col_off = tap_index % 3
        conv_sum = conv_sum + jnp.einsum('shwi,sio->shwo', padded[:, row_off:row_off + RES, col_off:col_off + RES], kernels[:, tap_index], precision=HIGH)
    conv_raw = low_back(conv_sum.reshape(SLOTS, PIX, D))
    pre_act = conv_raw * demodulate[:, None, :] + conv_vecs[0] * noise_map[:, :, None] + conv_vecs[1]
    stream = leaky_relu(pre_act)
    input_low = low(stream)
    queries = low_back(low(jnp.einsum('spi,io->spo', input_low, w_qkv[0], precision=HIGH))).reshape(SLOTS, PIX, HEADS, DH)
    keyset = queries
    values_all = low_back(low(jnp.einsum('spi,io->spo', input_low, w_qkv[1], precision=HIGH))).reshape(SLOTS, PIX, HEADS, DH)
    products = jnp.einsum('sphd,sqhd->shpq', queries, keyset, precision=HIGH)
    key_square = lax.optimization_barrier(jnp.sum(keyset * keyset, axis=-1))
    scores = low_back((2.0 * products - jnp.transpose(key_square, (0, 2, 1))[:, :, None, :]) * score_scale)
    probs = low(jax.nn.softmax(scores, axis=-1))
    attended = low_back(low(jnp.einsum('shpq,sqhd->sphd', probs, values_all, precision=HIGH))).reshape(SLOTS, PIX, D)
    stream = stream + low_back(jnp.einsum('spc,cd->spd', attended, w_attn_out, precision=HIGH))
    class_rows = jnp.take(class_table, labels, axis=0)
    tokens = low(context + class_rows[:, None, :])
    ckeys = low_back(low(jnp.einsum('sci,io->sco', tokens, w_cross_kv[0], precision=HIGH))).reshape(SLOTS, CT, HEADS, DH)
    cvalues = low_back(low(jnp.einsum('sci,io->sco', tokens, w_cross_kv[1], precision=HIGH))).reshape(SLOTS, CT, HEADS, DH)
    cqueries = low_back(low(jnp.einsum('spi,io->spo', low(stream), w_cross_q, precision=HIGH))).reshape(SLOTS, PIX, HEADS, DH)
    cscores = low_back(jnp.einsum('sphd,schd->shpc', cqueries, ckeys, precision=HIGH) * score_scale)
    cprobs = low(jax.nn.softmax(cscores, axis=-1))
    cout = low_back(low(jnp.einsum('shpc,schd->sphd', cprobs, cvalues, precision=HIGH))).reshape(SLOTS, PIX, D)
    stream = stream + low_back(jnp.einsum('spc,cd->spd', cout, w_cross_out, precision=HIGH))
    hidden = low_back(jnp.einsum('spi,if->spf', low(stream), w_mlp_in, precision=HIGH))
    active = low(jax.nn.gelu(hidden, approximate=True))
    stream = stream + low_back(jnp.einsum('spf,fd->spd', active, w_mlp_out, precision=HIGH))
    colour = jnp.einsum('spi,ci->scp', low(stream), w_rgb, precision=HIGH)
    return (stream, colour)

def reference(features, style_code, labels, counts, context, noise_map, w_select, w_mod, kernel_bank, conv_vecs, class_table, w_qkv, w_attn_out, w_cross_q, w_cross_kv, w_cross_out, w_mlp_in, w_mlp_out, w_rgb, cot_feat, cot_rgb):
    weights = (w_select.astype(jnp.float32), w_mod.astype(jnp.float32), kernel_bank.astype(jnp.float32), conv_vecs.astype(jnp.float32), class_table.astype(jnp.float32), w_qkv.astype(jnp.float32), w_attn_out.astype(jnp.float32), w_cross_q.astype(jnp.float32), w_cross_kv.astype(jnp.float32), w_cross_out.astype(jnp.float32), w_mlp_in.astype(jnp.float32), w_mlp_out.astype(jnp.float32), w_rgb.astype(jnp.float32))

    def split_groups(array):
        return array.reshape((GROUPS, SLOTS) + array.shape[1:])
    feats_in = split_groups(features.astype(jnp.float32))
    style_in = split_groups(style_code.astype(jnp.float32))
    labels_in = split_groups(labels.astype(jnp.int32))
    context_in = split_groups(context.astype(jnp.float32))
    noise_in = split_groups(noise_map.astype(jnp.float32))
    slot_ids = jnp.arange(SLOTS, dtype=jnp.int32)[None, :]
    live = (slot_ids < counts.astype(jnp.int32)[:, None]).astype(jnp.float32)
    factor = live / counts[:, None].astype(jnp.float32)

    def whole(weight_tuple, feats):

        def per_block(item):
            return block_forward(weight_tuple, item)
        return lax.map(jax.checkpoint(per_block), (feats, style_in, labels_in, context_in, noise_in))
    (streams, colours), pullback = jax.vjp(whole, weights, feats_in)
    cot_stream = split_groups(cot_feat.astype(jnp.float32)) * factor[:, :, None, None]
    cot_colour = split_groups(cot_rgb.astype(jnp.float32)) * factor[:, :, None, None]
    grad_weights, grad_feats = pullback((cot_stream, cot_colour))
    features_out = (streams * live[:, :, None, None]).reshape(BS, PIX, D).astype(jnp.bfloat16)
    rgb_out = (colours * live[:, :, None, None]).reshape(BS, 3, PIX).astype(jnp.bfloat16)
    grad_input = grad_feats.reshape(BS, PIX_IN, D)
    return (features_out, rgb_out, grad_input, grad_weights[0], grad_weights[1], grad_weights[2], grad_weights[3], grad_weights[4], grad_weights[5], grad_weights[6], grad_weights[7], grad_weights[8], grad_weights[9], grad_weights[10], grad_weights[11], grad_weights[12])
```

```python
from functools import partial

import jax
import jax.numpy as jnp
from jax import lax
from jax.experimental import pallas as pl
from jax.experimental.pallas import tpu as pltpu
from jax.sharding import PartitionSpec as P

DH = 64
CH = 16
RES = 16
HALF = RES // 2
LOW = HALF * HALF
PIX = RES * RES
EXTRA = 16
HIGH = lax.Precision.HIGHEST
ROOT_TWO = 1.4142135623730951
SLOPE = 0.2
DEMOD_EPS = 1e-08
BF = jnp.bfloat16
F32 = jnp.float32


def dot32(spec, *args):
    return jnp.einsum(spec, *args, preferred_element_type=F32)


def split_heads(array):
    return array.reshape(array.shape[:-1] + (array.shape[-1] // DH, DH))


def join_heads(array):
    return array.reshape(array.shape[:-2] + (array.shape[-2] * array.shape[-1],))


def hi_lo(value):
    high = value.astype(BF)
    return high, (value - high.astype(F32)).astype(BF)


def mix_body(blocks, mix_ref, bank_ref, mod2_ref, kern_ref, sums_ref):
    count = kern_ref.shape[0]
    wide = kern_ref.shape[3]

    @pl.when(pl.program_id(0) == 0)
    def _():
        sums_ref[...] = jnp.zeros_like(sums_ref)

    total = jnp.zeros((count, wide), F32)
    for block in range(blocks):
        rows = slice(block * CH, (block + 1) * CH)
        part = bank_ref[:, 0, rows, :].reshape(-1, wide)
        low = jnp.dot(mix_ref[...], part, preferred_element_type=F32).astype(BF)
        kern_ref[:, 0, rows, :] = low.reshape(count, CH, wide)
        full = low.astype(F32)
        square = full * full * mod2_ref[block]
        total = total + jnp.sum(square.reshape(count, CH, wide), axis=1)
    sums_ref[...] += total


def mix_kernels(mix_wide, bank, mod2_cols):
    kinds, taps, deep, wide = bank.shape
    count = mix_wide.shape[0] // CH
    return pl.pallas_call(
        partial(mix_body, deep // CH),
        grid=(taps,),
        in_specs=[
            pl.BlockSpec(mix_wide.shape, lambda t: (0, 0)),
            pl.BlockSpec((kinds, 1, deep, wide), lambda t: (0, t, 0, 0)),
            pl.BlockSpec(mod2_cols.shape, lambda t: (0, 0, 0)),
        ],
        out_specs=[
            pl.BlockSpec((count, 1, deep, wide), lambda t: (0, t, 0, 0)),
            pl.BlockSpec((count, wide), lambda t: (0, 0)),
        ],
        out_shape=[
            jax.ShapeDtypeStruct((count, taps, deep, wide), BF),
            jax.ShapeDtypeStruct((count, wide), F32),
        ],
        compiler_params=pltpu.CompilerParams(vmem_limit_bytes=48 << 20),
        name="mix_kernels",
    )(mix_wide, bank, mod2_cols)


def conv_body(win_ref, kern_ref, sums_ref, out_ref):
    deep = win_ref.shape[4]
    wide = kern_ref.shape[3]

    def window(tap):
        row_off, col_off = tap // 3, tap % 3
        rows = [win_ref[0, col_off, (y + row_off - 1) // 2 + 1] for y in range(RES)]
        return jnp.concatenate(rows, axis=0)

    if deep % 128 == 0:
        wins = jnp.concatenate([window(tap) for tap in range(9)], axis=1)
        total = jnp.dot(wins, kern_ref[0].reshape(9 * deep, wide), preferred_element_type=F32)
    else:
        total = jnp.zeros((PIX, wide), F32)
        for tap in range(9):
            total = total + jnp.dot(window(tap), kern_ref[0, tap], preferred_element_type=F32)
    out_ref[0, :PIX] = total.astype(BF)
    high = sums_ref[0].astype(BF).astype(F32)
    low = sums_ref[0] - high
    row = lax.broadcasted_iota(jnp.int32, (EXTRA, wide), 0)
    out_ref[0, PIX:] = jnp.where(row == 0, high, jnp.where(row == 1, low, 0.0)).astype(BF)


def conv_forward(windows, kernels, sums):
    count, taps, deep, wide = kernels.shape
    return pl.pallas_call(
        conv_body,
        grid=(count,),
        in_specs=[
            pl.BlockSpec((1,) + windows.shape[1:], lambda s: (s, 0, 0, 0, 0)),
            pl.BlockSpec((1, taps, deep, wide), lambda s: (s, 0, 0, 0)),
            pl.BlockSpec((1, 1, wide), lambda s: (s, 0, 0)),
        ],
        out_specs=pl.BlockSpec((1, PIX + EXTRA, wide), lambda s: (s, 0, 0)),
        out_shape=jax.ShapeDtypeStruct((count, PIX + EXTRA, wide), BF),
        compiler_params=pltpu.CompilerParams(vmem_limit_bytes=48 << 20),
        name="conv_forward",
    )(windows, kernels, sums[:, None, :])


def conv_back_body(
    order_ref, dconv_ref, kern_ref, turned_ref, mod2_ref, mod_ref, feat_ref, dkern_ref, dgrid_ref, dmod_ref
):
    deep, wide = kern_ref.shape[2], kern_ref.shape[3]
    grads = dconv_ref[0, 0, :PIX].astype(F32).reshape(RES, 2, HALF, wide)
    dsq = dconv_ref[0, 0, PIX:].astype(F32)
    dsq = jnp.sum(dsq, axis=0, keepdims=True)
    even, odd = grads[:, 0], grads[:, 1]
    none = jnp.zeros((RES, 1, wide), F32)
    after = jnp.concatenate([even[:, 1:], none], axis=1)
    before = jnp.concatenate([none, odd[:, :-1]], axis=1)
    by_col = (odd + after, even + odd, before + even)
    gap = jnp.zeros((1, HALF, wide), F32)
    into = jnp.zeros((2 * LOW, deep), F32)
    squares = jnp.zeros((deep, wide), F32)
    scaled = 2.0 * mod2_ref[0] * dsq
    for col_off in range(3):
        rows = by_col[col_off].reshape(HALF, 2, HALF, wide)
        first, second = rows[:, 0], rows[:, 1]
        by_row = (
            second + jnp.concatenate([first[1:], gap], axis=0),
            first + second,
            jnp.concatenate([gap, second[:-1]], axis=0) + first,
        )
        for row_off in range(3):
            tap = 3 * row_off + col_off
            exact = by_row[row_off].reshape(LOW, wide)
            high = exact.astype(BF)
            low = (exact - high.astype(F32)).astype(BF)
            both = jnp.concatenate([high, low], axis=0)
            kern = kern_ref[0, tap]
            full = kern.astype(F32)
            grad = jnp.dot(turned_ref[0], both, preferred_element_type=F32)
            dkern_ref[0, tap] = (grad + full * scaled).astype(BF)
            squares = squares + full * full
            into = into + lax.dot_general(
                both, kern, (((1,), (1,)), ((), ())), preferred_element_type=F32
            )
    dlow = into[:LOW] + into[LOW:]
    dgrid_ref[0] = dlow * mod_ref[0]
    direct = jnp.sum(dlow * feat_ref[0].astype(F32), axis=0, keepdims=True)
    through = lax.dot_general(
        jnp.broadcast_to(dsq, (8, wide)),
        squares,
        (((1,), (1,)), ((), ())),
        precision=HIGH,
        preferred_element_type=F32,
    )
    dmod_ref[0] = direct + 2.0 * mod_ref[0] * through[:1]


def conv_backward(order, dconv, kernels, turned, mod2_col, modulate, feats):
    count, taps, deep, wide = kernels.shape
    slots = dconv.shape[1]
    grid_spec = pltpu.PrefetchScalarGridSpec(
        num_scalar_prefetch=1,
        grid=(count,),
        in_specs=[
            pl.BlockSpec((1, 1, PIX + EXTRA, wide), lambda s, o: (o[s // slots], s % slots, 0, 0)),
            pl.BlockSpec((1, taps, deep, wide), lambda s, o: (s, 0, 0, 0)),
            pl.BlockSpec((1, deep, 2 * LOW), lambda s, o: (s, 0, 0)),
            pl.BlockSpec((1, deep, 1), lambda s, o: (s, 0, 0)),
            pl.BlockSpec((1, 1, deep), lambda s, o: (s, 0, 0)),
            pl.BlockSpec((1, LOW, deep), lambda s, o: (s, 0, 0)),
        ],
        out_specs=[
            pl.BlockSpec((1, taps, deep, wide), lambda s, o: (s, 0, 0, 0)),
            pl.BlockSpec((1, LOW, deep), lambda s, o: (s, 0, 0)),
            pl.BlockSpec((1, 1, deep), lambda s, o: (s, 0, 0)),
        ],
    )
    return pl.pallas_call(
        conv_back_body,
        grid_spec=grid_spec,
        out_shape=[
            jax.ShapeDtypeStruct((count, taps, deep, wide), BF),
            jax.ShapeDtypeStruct((count, LOW, deep), F32),
            jax.ShapeDtypeStruct((count, 1, deep), F32),
        ],
        compiler_params=pltpu.CompilerParams(vmem_limit_bytes=48 << 20),
        name="conv_backward",
    )(order, dconv, kernels, turned, mod2_col, modulate, feats)


def bank_back_body(blocks, mix_ref, dkern_ref, bank_ref, gbank_ref, cross_ref):
    wide = bank_ref.shape[3]

    @pl.when(pl.program_id(0) == 0)
    def _():
        cross_ref[...] = jnp.zeros_like(cross_ref)

    total = jnp.zeros(cross_ref.shape, F32)
    for block in range(blocks):
        rows = slice(block * CH, (block + 1) * CH)
        grads = dkern_ref[:, 0, rows, :].reshape(-1, wide)
        part = bank_ref[:, 0, rows, :].reshape(-1, wide)
        out = jnp.dot(mix_ref[...], grads, preferred_element_type=F32)
        gbank_ref[:, 0, rows, :] = out.reshape(-1, CH, wide)
        total = total + lax.dot_general(
            grads, part, (((1,), (1,)), ((), ())), preferred_element_type=F32
        )
    cross_ref[...] += total


def bank_backward(mix_wide_t, dkernels, bank):
    kinds, taps, deep, wide = bank.shape
    count = dkernels.shape[0]
    return pl.pallas_call(
        partial(bank_back_body, deep // CH),
        grid=(taps,),
        in_specs=[
            pl.BlockSpec(mix_wide_t.shape, lambda t: (0, 0)),
            pl.BlockSpec((count, 1, deep, wide), lambda t: (0, t, 0, 0)),
            pl.BlockSpec((kinds, 1, deep, wide), lambda t: (0, t, 0, 0)),
        ],
        out_specs=[
            pl.BlockSpec((kinds, 1, deep, wide), lambda t: (0, t, 0, 0)),
            pl.BlockSpec((count * CH, kinds * CH), lambda t: (0, 0)),
        ],
        out_shape=[
            jax.ShapeDtypeStruct(bank.shape, F32),
            jax.ShapeDtypeStruct((count * CH, kinds * CH), F32),
        ],
        compiler_params=pltpu.CompilerParams(vmem_limit_bytes=48 << 20),
        name="bank_backward",
    )(mix_wide_t, dkernels, bank)


class Exchange:
    def __init__(self, n_dp, n_h):
        self.n_dp, self.n_h = n_dp, n_h
        self.dp, self.head = lax.axis_index("dp"), lax.axis_index("head")

    def hop_head(self, x, step):
        return lax.ppermute(x, "head", [(i, i ^ step) for i in range(self.n_h)])

    def hop_dp(self, x, step):
        return lax.ppermute(x, "dp", [(i, i ^ step) for i in range(self.n_dp)])

    def gather_head(self, x):
        far = self.hop_head(x, 2)
        near = self.hop_head(x, 1)
        return [x, near, far, self.hop_head(far, 1)]

    def in_order(self, pieces):
        bit = (self.head & 1) == 1
        p, q, s, t = pieces
        p, q, s, t = (
            jnp.where(bit, q, p),
            jnp.where(bit, p, q),
            jnp.where(bit, t, s),
            jnp.where(bit, s, t),
        )
        bit = (self.head & 2) == 2
        return [
            jnp.where(bit, s, p),
            jnp.where(bit, t, q),
            jnp.where(bit, p, s),
            jnp.where(bit, q, t),
        ]

    def reduce_head(self, parts):
        send = jnp.stack([parts[1].astype(BF), parts[3].astype(BF)])
        got = self.hop_head(send, 1).astype(F32)
        other = self.hop_head((parts[2] + got[1]).astype(BF), 2)
        return parts[0] + got[0] + other.astype(F32)

    def reduce_dp(self, parts):
        if self.n_dp != 8:
            got = lax.all_to_all(parts, "dp", 0, 0, tiled=True)
            return jnp.sum(got.astype(F32), axis=0)
        y, z = self.dp & 1, self.dp >> 1
        pairs = parts.reshape((4, 2) + parts.shape[1:])
        keep = lax.dynamic_index_in_dim(pairs, y, 1, keepdims=False)
        send = lax.dynamic_index_in_dim(pairs, 1 - y, 1, keepdims=False)
        total = keep.astype(F32) + self.hop_dp(send, 1).astype(F32)
        out = lax.dynamic_index_in_dim(total, z, 0, keepdims=False)
        low = total.astype(BF)
        for step in (1, 2, 3):
            piece = lax.dynamic_index_in_dim(low, z ^ step, 0, keepdims=False)
            out = out + self.hop_dp(piece, 2 * step).astype(F32)
        return out

    def gather_dp(self, x):
        if self.n_dp != 8:
            return lax.all_gather(x, "dp", axis=0)
        return jnp.stack([x] + [self.hop_dp(x, k) for k in range(1, 8)])

    def order_dp(self):
        ranks = jnp.arange(self.n_dp, dtype=jnp.int32)
        return ranks ^ self.dp.astype(jnp.int32) if self.n_dp == 8 else ranks


def log_norm(scores):
    highest = jnp.max(scores, axis=-1, keepdims=True)
    return highest + jnp.log(jnp.sum(jnp.exp(scores - highest), axis=-1, keepdims=True))


def softmax_back(probs_full, dprobs):
    return probs_full * (dprobs - jnp.sum(probs_full * dprobs, axis=-1, keepdims=True))


def l2_scores(queries, keyset, score_scale):
    products = dot32("sphd,sqhd->shpq", queries, keyset)
    key_square = jnp.sum(jnp.square(keyset.astype(F32)), axis=-1)
    return (2.0 * products - jnp.transpose(key_square, (0, 2, 1))[:, :, None, :]) * score_scale


def on_device(
    n_dp,
    n_h,
    features,
    style_code,
    labels,
    counts,
    context,
    noise_map,
    w_select,
    w_mod,
    kernel_bank,
    conv_vecs,
    class_table,
    w_qkv,
    w_attn_out,
    w_cross_q,
    w_cross_kv,
    w_cross_out,
    w_mlp_in,
    w_mlp_out,
    w_rgb,
    cot_feat,
    cot_rgb,
):
    ex = Exchange(n_dp, n_h)
    slots, own_low, wide_all = features.shape
    kinds, taps, deep, wide = kernel_bank.shape
    own_pix = cot_feat.shape[1]
    count = n_dp * slots
    style_rows = w_select.shape[0]
    style_width = style_code.shape[1]
    hidden_own = w_mlp_in.shape[1]
    score_scale = DH ** (-0.5)

    label_parts = jnp.stack([labels // 256, labels % 256]).astype(BF)
    small = jnp.concatenate(
        [
            style_code.reshape(-1),
            w_select.reshape(-1),
            conv_vecs.reshape(-1),
            w_rgb.reshape(-1),
            label_parts.reshape(-1),
        ]
    )
    small_all = lax.all_gather(small, "dp", axis=0)
    sizes = [style_code.size, w_select.size, conv_vecs.size, w_rgb.size, label_parts.size]
    pieces, at = [], 0
    for size in sizes:
        pieces.append(small_all[:, at : at + size])
        at += size
    style_all = pieces[0].reshape(count, style_width)
    select_full = pieces[1].reshape(style_width, kinds)
    vecs_full = pieces[2].reshape(n_dp, 2, deep).transpose(1, 0, 2).reshape(2, wide_all)
    rgb_full = pieces[3].reshape(n_dp, 3, deep).transpose(1, 0, 2).reshape(3, wide_all)
    labels_all = pieces[4].reshape(n_dp, 2, slots).astype(jnp.int32)
    labels_all = (labels_all[:, 0] * 256 + labels_all[:, 1]).reshape(count)

    feats = lax.all_to_all(features, "dp", 2, 0, tiled=True)
    feats = lax.all_gather(feats, "head", axis=1, tiled=True)
    mod_cols = lax.all_to_all(w_mod, "dp", 1, 0, tiled=True)

    first = jnp.concatenate(
        [
            w_qkv.reshape(-1, wide),
            w_cross_kv.reshape(-1, wide),
            w_cross_q,
        ],
        axis=0,
    )
    second = jnp.concatenate([w_attn_out, w_cross_out], axis=1)
    first_all = lax.all_gather(first, "dp", axis=0)
    second_all = lax.all_gather(second, "dp", axis=0)
    mlp_pack = jnp.concatenate([w_mlp_in, w_mlp_out.T], axis=0)
    mlp_all = lax.all_gather(mlp_pack, "dp", axis=0)

    qkv_full = first_all[:, : 2 * deep].reshape(n_dp, 2, deep, wide).transpose(1, 0, 2, 3).reshape(2, wide_all, wide)
    cross_kv_full = first_all[:, 2 * deep : 4 * deep].reshape(n_dp, 2, deep, wide).transpose(1, 0, 2, 3).reshape(2, wide_all, wide)
    cross_q_own = first_all[:, 4 * deep :].reshape(wide_all, wide)
    attn_own = second_all[:, :, :deep].transpose(1, 0, 2).reshape(wide, wide_all)
    cross_out_own = second_all[:, :, deep:].transpose(1, 0, 2).reshape(wide, wide_all)
    mlp_in_own = mlp_all[:, :deep].reshape(wide_all, hidden_own)
    mlp_out_own_t = mlp_all[:, deep:].reshape(wide_all, hidden_own)
    attn_full = jnp.concatenate(ex.in_order(ex.gather_head(attn_own)), axis=0)
    cross_out_full = jnp.concatenate(ex.in_order(ex.gather_head(cross_out_own)), axis=0)
    cross_q_full = jnp.concatenate(ex.in_order(ex.gather_head(cross_q_own)), axis=1)

    mixing = jax.nn.softmax(jnp.dot(style_all, select_full, preferred_element_type=F32), axis=-1)
    mixing_low = mixing.astype(BF)
    unit = jnp.eye(CH, dtype=BF)
    mix_wide = (mixing_low[:, None, :, None] * unit[None, :, None, :]).reshape(count * CH, kinds * CH)
    modulate = 1.0 + jnp.dot(style_all, mod_cols, preferred_element_type=F32)
    mod2 = jnp.square(modulate)
    mod2_cols = mod2.reshape(count, deep // CH, CH).transpose(1, 0, 2).reshape(deep // CH, count * CH, 1)
    kernels, square_part = mix_kernels(mix_wide, kernel_bank, mod2_cols)
    mod_low = (feats.astype(F32) * modulate[:, None, :]).astype(BF)
    grid = jnp.repeat(mod_low.reshape(count, HALF, HALF, deep), 2, axis=2)
    grid = jnp.pad(grid, ((0, 0), (1, 1), (1, 1), (0, 0)))
    windows = jnp.stack([grid[:, :, b : b + RES] for b in range(3)], axis=1)
    conv_part = conv_forward(windows, kernels, square_part)
    conv_got = lax.all_to_all(
        conv_part.reshape(n_dp, slots, PIX + EXTRA, wide), "dp", 0, 0, tiled=True
    )
    conv_sum = jnp.sum(conv_got.astype(F32), axis=0)
    conv_raw = conv_sum[:, :PIX]
    demodulate = lax.rsqrt(conv_sum[:, PIX] + conv_sum[:, PIX + 1] + DEMOD_EPS)

    vecs_own = lax.dynamic_slice_in_dim(vecs_full, ex.head * wide, wide, 1).astype(F32)
    noise_full = noise_map.astype(F32)
    pre_act = conv_raw * demodulate[:, None, :] + vecs_own[0] * noise_full[:, :, None] + vecs_own[1]
    stream_cols = jnp.where(pre_act > 0, pre_act, SLOPE * pre_act) * ROOT_TWO
    cols_high, cols_low = hi_lo(stream_cols)
    full0 = jnp.concatenate(ex.in_order(ex.gather_head(cols_high)), axis=2)
    own_start = ex.head * own_pix
    stream0 = lax.dynamic_slice_in_dim(full0, own_start, own_pix, 1).astype(F32) + lax.all_to_all(
        cols_low, "head", 1, 2, tiled=True
    ).astype(F32)

    qkv_own = dot32("spi,nio->nspo", full0, qkv_full).astype(BF)
    queries, values_all = split_heads(qkv_own[0]), split_heads(qkv_own[1])
    scores = l2_scores(queries, queries, score_scale)
    self_norm = log_norm(scores)
    probs_low = jnp.exp(scores - self_norm).astype(BF)
    attended = join_heads(dot32("shpq,sqhd->sphd", probs_low, values_all).astype(BF))
    attended_pix = lax.all_to_all(attended, "head", 1, 2, tiled=True)
    stream1 = stream0 + dot32("spc,cd->spd", attended_pix, attn_full)
    low1 = stream1.astype(BF)

    table_rows = class_table.shape[0]
    one_hot = (
        labels_all[:, None] == ex.dp * table_rows + jnp.arange(table_rows, dtype=jnp.int32)[None, :]
    )
    class_part = jnp.dot(one_hot.astype(BF), class_table, preferred_element_type=F32).astype(BF)
    class_got = lax.all_to_all(class_part.reshape(n_dp, slots, wide_all), "dp", 0, 0, tiled=True)
    class_rows = jnp.sum(class_got.astype(F32), axis=0)
    tokens = (context.astype(F32) + class_rows[:, None, :]).astype(BF)
    cross_kv_own = dot32("sci,nio->nsco", tokens, cross_kv_full).astype(BF)
    cross_kv_heads = lax.all_gather(cross_kv_own, "head", axis=3, tiled=True)
    ckeys, cvalues = split_heads(cross_kv_heads[0]), split_heads(cross_kv_heads[1])

    cqueries = split_heads(dot32("spi,io->spo", low1, cross_q_full).astype(BF))
    cscores = dot32("sphd,schd->shpc", cqueries, ckeys) * score_scale
    cross_norm = log_norm(cscores)
    cprobs_full = jnp.exp(cscores - cross_norm)
    cprobs_low = cprobs_full.astype(BF)
    cout = join_heads(dot32("shpc,schd->sphd", cprobs_low, cvalues).astype(BF))
    stream2 = stream1 + dot32("spc,cd->spd", cout, cross_out_full)

    full2 = jnp.stack(ex.gather_head(stream2.astype(BF)))
    hidden = dot32("kspi,if->kspf", full2, mlp_in_own)
    active = jax.nn.gelu(hidden, approximate=True).astype(BF)
    stream3 = stream2 + ex.reduce_head(dot32("kspf,df->kspd", active, mlp_out_own_t))

    live_slots = (jnp.arange(slots, dtype=jnp.int32) < counts[0]).astype(F32)
    factor = live_slots / counts[0].astype(F32)
    features_out = (stream3 * live_slots[:, None, None]).astype(BF)
    final_low = stream3.astype(BF)
    colour = dot32("spi,ci->scp", final_low, rgb_full)
    rgb_out = (colour * live_slots[:, None, None]).astype(BF)
    dcolour = cot_rgb.astype(F32) * factor[:, None, None]
    dstream = cot_feat.astype(F32) * factor[:, None, None] + jnp.einsum(
        "scp,ci->spi", dcolour, rgb_full.astype(F32), precision=HIGH
    )
    rgb_part = jnp.einsum("scp,spi->ci", dcolour, final_low.astype(F32), precision=HIGH)

    dbranch = jnp.stack(ex.gather_head(dstream.astype(BF)))
    dactive = dot32("kspd,df->kspf", dbranch, mlp_out_own_t)
    _, gelu_pull = jax.vjp(partial(jax.nn.gelu, approximate=True), hidden)
    dhidden = gelu_pull(dactive)[0].astype(BF)
    dstream = dstream + ex.reduce_head(dot32("kspf,if->kspi", dhidden, mlp_in_own))
    mlp_out_grad = dot32("kspf,kspnd->nfd", active, dbranch.reshape(dbranch.shape[:3] + (n_dp, deep)))
    mlp_in_grad = dot32("kspi,kspf->if", full2, dhidden).reshape(n_dp, deep, hidden_own)
    grad_mlp_out = ex.reduce_dp(mlp_out_grad.astype(BF))
    grad_mlp_in = ex.reduce_dp(mlp_in_grad.astype(BF))

    dcross = dstream.astype(BF)
    dcout = split_heads(dot32("spd,cd->spc", dcross, cross_out_full).astype(BF))
    dcprobs = dot32("sphd,schd->shpc", dcout, cvalues)
    dcvalues_part = dot32("shpc,sphd->schd", cprobs_low, dcout)
    dcscores = softmax_back(cprobs_full, dcprobs).astype(BF)
    dcqueries = join_heads((dot32("shpc,schd->sphd", dcscores, ckeys) * score_scale).astype(BF))
    dckeys_part = dot32("shpc,sphd->schd", dcscores, cqueries) * score_scale
    dstream = dstream + dot32("spo,io->spi", dcqueries, cross_q_full)
    dkv_part = jnp.stack([join_heads(dckeys_part), join_heads(dcvalues_part)])
    dkv_got = lax.all_to_all(dkv_part.reshape(dkv_part.shape[:-1] + (n_h, wide)), "head", 3, 0, tiled=False)
    dcross_kv = jnp.sum(dkv_got, axis=0).astype(BF)
    cross_kv_grad = dot32("sci,nsco->nio", tokens, dcross_kv)
    dtokens_sum = jnp.sum(dot32("nsco,nio->sci", dcross_kv, cross_kv_full), axis=1)
    swapped = lax.all_to_all(jnp.stack([dcqueries, cout]), "head", 3, 2, tiled=True)
    dcq_cols, cout_cols = swapped[0], swapped[1]
    full1 = lax.all_gather(low1, "head", axis=1, tiled=True)
    dcross_all = lax.all_gather(dcross, "head", axis=1, tiled=True)
    cross_q_grad = dot32("spi,spo->io", full1, dcq_cols)
    cross_out_grad = dot32("spc,spnd->ncd", cout_cols, dcross_all.reshape(slots, PIX, n_dp, deep))
    grad_cross_out = ex.reduce_dp(cross_out_grad.astype(BF))
    grad_cross_q = ex.reduce_dp(cross_q_grad.astype(BF).reshape(n_dp, deep, wide))
    grad_cross_kv = ex.reduce_dp(
        cross_kv_grad.astype(BF).reshape(2, n_dp, deep, wide).transpose(1, 0, 2, 3)
    )

    dattn = dstream.astype(BF)
    dattended = dot32("spd,cd->spc", dattn, attn_full).astype(BF)
    dattended = split_heads(lax.all_to_all(dattended, "head", 2, 1, tiled=True))
    dattn_all = lax.all_gather(dattn, "head", axis=1, tiled=True)
    attn_out_grad = dot32("spc,spnd->ncd", attended, dattn_all.reshape(slots, PIX, n_dp, deep))
    grad_attn_out = ex.reduce_dp(attn_out_grad.astype(BF))
    dstream_cols = lax.all_to_all(dattn, "head", 2, 1, tiled=True)
    probs_full = jnp.exp(scores - self_norm)
    dprobs = dot32("sphd,sqhd->shpq", dattended, values_all)
    dvalues = dot32("shpq,sphd->sqhd", probs_low, dattended).astype(BF)
    dscores = softmax_back(probs_full, dprobs).astype(BF)
    column_sums = jnp.transpose(jnp.sum(dscores.astype(F32), axis=2), (0, 2, 1))
    as_query = dot32("shpq,sqhd->sphd", dscores, queries)
    as_key = dot32("shpq,sphd->sqhd", dscores, queries)
    dshared = (
        (as_query + as_key - queries.astype(F32) * column_sums[..., None]) * (2.0 * score_scale)
    ).astype(BF)
    dqkv = jnp.stack((join_heads(dshared), join_heads(dvalues)), axis=0)
    qkv_blocks = qkv_full.reshape(2, n_h, wide, wide)
    parts = [
        dot32(
            "nspo,nio->spi",
            dqkv,
            lax.dynamic_index_in_dim(qkv_blocks, ex.head ^ k, 1, keepdims=False),
        )
        for k in range(n_h)
    ]
    dconv_out = dstream_cols.astype(F32) + ex.reduce_head(parts)
    qkv_grad = dot32("spi,nspo->nio", full0, dqkv).astype(BF)
    grad_qkv = ex.reduce_dp(qkv_grad.reshape(2, n_dp, deep, wide).transpose(1, 0, 2, 3))

    dpre = dconv_out * ROOT_TWO * jnp.where(pre_act > 0, 1.0, SLOPE)
    vecs_part = jnp.stack(
        [jnp.sum(dpre * noise_full[:, :, None], axis=(0, 1)), jnp.sum(dpre, axis=(0, 1))]
    )
    ddemod = jnp.sum(dpre * conv_raw, axis=1)
    dsquare = ddemod * -0.5 * demodulate * demodulate * demodulate
    dconv = (dpre * demodulate[:, None, :]).astype(BF)
    dconv = dconv.reshape(slots, RES, HALF, 2, wide).transpose(0, 1, 3, 2, 4).reshape(slots, PIX, wide)
    dsq_high, dsq_low = hi_lo(dsquare)
    extra = jnp.pad(jnp.stack([dsq_high, dsq_low], axis=1), ((0, 0), (0, EXTRA - 2), (0, 0)))
    dconv_all = ex.gather_dp(jnp.concatenate([dconv, extra], axis=1))
    turned = mod_low.transpose(0, 2, 1)
    turned = jnp.concatenate([turned, turned], axis=2)
    dkernels, dgrid, dmod = conv_backward(
        ex.order_dp(), dconv_all, kernels, turned, mod2[:, :, None], modulate[:, None, :], feats
    )
    grad_bank, cross = bank_backward(mix_wide.T, dkernels, kernel_bank)
    dmixing_part = jnp.einsum("saka->sk", cross.reshape(count, CH, kinds, CH))

    pieces_in = dgrid.reshape(n_dp, slots, n_h, own_low, deep).transpose(0, 2, 1, 3, 4)
    pieces_in = pieces_in.reshape(n_dp * n_h, slots * own_low * deep)
    got = lax.all_to_all(pieces_in, ("dp", "head"), 0, 0, tiled=True)
    grad_input = jnp.sum(got.reshape(n_dp, n_h, slots, own_low, deep), axis=1)
    grad_input = grad_input.transpose(1, 2, 0, 3).reshape(slots, own_low, wide_all)

    tail = jnp.concatenate([dmod[:, 0, :].reshape(-1), dmixing_part.reshape(-1)])
    tail = lax.all_gather(tail, ("dp", "head"), axis=0).reshape(n_dp, n_h, -1)
    dmodulate = jnp.sum(tail[:, :, : count * deep], axis=1).reshape(n_dp, count, deep)
    dmodulate = dmodulate.transpose(1, 0, 2).reshape(count, wide_all)
    dmixing = jnp.sum(tail[:, :, count * deep :], axis=(0, 1)).reshape(count, kinds)
    style_own = lax.dynamic_slice_in_dim(style_all, ex.dp * style_rows, style_rows, 1).astype(F32)
    grad_mod = jnp.einsum("sr,sc->rc", style_own, dmodulate, precision=HIGH)
    logit_grad = mixing * (dmixing - jnp.sum(mixing * dmixing, axis=-1, keepdims=True))
    grad_select = jnp.einsum("sr,sk->rk", style_own, logit_grad, precision=HIGH)

    early = jnp.concatenate([rgb_part.reshape(-1), dtokens_sum.reshape(-1), vecs_part.reshape(-1)])
    early = lax.all_gather(early, ("dp", "head"), axis=0).reshape(n_dp, n_h, -1)
    at = 3 * wide_all
    rgb_sum = jnp.sum(early[:, :, :at], axis=(0, 1)).reshape(3, wide_all)
    grad_rgb = lax.dynamic_slice_in_dim(rgb_sum, ex.dp * deep, deep, 1)
    dtok_all = jnp.sum(early[:, :, at : at + slots * wide_all], axis=1).reshape(count, wide_all)
    grad_table = jnp.einsum("sr,sc->rc", one_hot.astype(F32), dtok_all, precision=HIGH)
    vecs_sum = jnp.sum(early[:, :, at + slots * wide_all :], axis=0).reshape(n_h, 2, wide)
    vecs_sum = vecs_sum.transpose(1, 0, 2).reshape(2, wide_all)
    grad_vecs = lax.dynamic_slice_in_dim(vecs_sum, ex.dp * deep, deep, 1)

    return (
        features_out,
        rgb_out,
        grad_input,
        grad_select,
        grad_mod,
        grad_bank,
        grad_vecs,
        grad_table,
        grad_qkv,
        grad_attn_out,
        grad_cross_q,
        grad_cross_kv,
        grad_cross_out,
        grad_mlp_in,
        grad_mlp_out,
        grad_rgb,
    )


def solution(mesh):
    return jax.shard_map(
        partial(on_device, mesh.shape["dp"], mesh.shape["head"]),
        mesh=mesh,
        in_specs=(
            P("dp", "head", None),
            P("dp", None),
            P("dp"),
            P("dp"),
            P("dp", None, None),
            P("dp", None),
            P("dp", None),
            P("dp", None),
            P(None, None, "dp", "head"),
            P(None, "dp"),
            P("dp", None),
            P(None, "dp", "head"),
            P("head", "dp"),
            P("dp", "head"),
            P(None, "dp", "head"),
            P("head", "dp"),
            P("dp", "head"),
            P("head", "dp"),
            P(None, "dp"),
            P("dp", "head", None),
            P("dp", None, "head"),
        ),
        out_specs=(
            P("dp", "head", None),
            P("dp", None, "head"),
            P("dp", "head", None),
            P("dp", None),
            P("dp", None),
            P(None, None, "dp", "head"),
            P(None, "dp"),
            P("dp", None),
            P(None, "dp", "head"),
            P("head", "dp"),
            P("dp", "head"),
            P(None, "dp", "head"),
            P("head", "dp"),
            P("dp", "head"),
            P("head", "dp"),
            P(None, "dp"),
        ),
        check_vma=False,
    )
```

```python
from functools import partial

import jax
import jax.numpy as jnp
import numpy as np
from jax import lax
from jax.experimental import pallas as pl
from jax.experimental.pallas import tpu as pltpu
from jax.sharding import PartitionSpec as P

DH = 64
CH = 16
RES = 16
HALF = RES // 2
LOW = HALF * HALF
PIX = RES * RES
EXTRA = 16
BLOCK = 128
HIGH = lax.Precision.HIGHEST
ROOT_TWO = 1.4142135623730951
SLOPE = 0.2
DEMOD_EPS = 1e-08
BF = jnp.bfloat16
F32 = jnp.float32


def dot32(spec, *args):
    return jnp.einsum(spec, *args, preferred_element_type=F32)


def split_heads(array):
    return array.reshape(array.shape[:-1] + (array.shape[-1] // DH, DH))


def join_heads(array):
    return array.reshape(array.shape[:-2] + (array.shape[-2] * array.shape[-1],))


def in_hbm(x):
    return pltpu.with_memory_space_constraint(x, pltpu.HBM)


def hi_lo(value):
    high = value.astype(BF)
    return high, (value - high.astype(F32)).astype(BF)


def pack_body(label_ref, style_ref, select_ref, vecs_ref, rgb_ref, mod_ref, feat_ref, out_ref, work_ref):
    work_ref[...] = jnp.zeros_like(work_ref)
    n_dp, _, lanes = out_ref.shape
    slots, style_width = style_ref.shape
    per = style_width // lanes
    for s in range(slots):
        for c in range(per):
            piece = style_ref[s : s + 1, c * lanes : (c + 1) * lanes]
            work_ref[s * per + c : s * per + c + 1, :] = piece.astype(F32)
    rows, kinds = select_ref.shape
    unit = lax.broadcasted_iota(jnp.int32, (rows, lanes), 0) == lax.broadcasted_iota(
        jnp.int32, (rows, lanes), 1
    )
    work_ref[8 : 8 + kinds, :] = dot_tn(select_ref[...].astype(F32), unit.astype(F32))
    work_ref[16:18, :] = vecs_ref[...].astype(F32)
    work_ref[18:21, :] = rgb_ref[...].astype(F32)
    lane = lax.broadcasted_iota(jnp.int32, (1, lanes), 1)
    row = jnp.zeros((1, lanes), jnp.int32)
    for s in range(slots):
        row = jnp.where(lane == s, label_ref[s] >> 8, row)
        row = jnp.where(lane == slots + s, label_ref[s] & 255, row)
    work_ref[21:22, :] = row.astype(F32)
    common = work_ref[...].astype(BF)
    for d in range(n_dp):
        cols = slice(d * lanes, (d + 1) * lanes)
        out_ref[d, :64] = mod_ref[:, cols]
        out_ref[d, 64:96] = feat_ref[:, cols]
        out_ref[d, 96:] = common


def pack_first(labels, style, select, vecs, rgb, mod, feats):
    lanes = vecs.shape[1]
    whole = pl.BlockSpec(memory_space=pltpu.VMEM)
    return pl.pallas_call(
        pack_body,
        in_specs=[pl.BlockSpec(memory_space=pltpu.SMEM)] + [whole] * 6,
        out_specs=whole,
        out_shape=jax.ShapeDtypeStruct((mod.shape[1] // lanes, 128, lanes), BF),
        scratch_shapes=[pltpu.VMEM((32, lanes), F32)],
        compiler_params=pltpu.CompilerParams(vmem_limit_bytes=8 << 20),
        name="pack_first",
    )(labels, style, select, vecs, rgb, mod, feats)


def pack_weights_body(qkv_ref, kv_ref, q_ref, attn_ref, out_ref, w_ref):
    wide = q_ref.shape[1]
    unit = lax.broadcasted_iota(jnp.int32, (wide, wide), 0) == lax.broadcasted_iota(
        jnp.int32, (wide, wide), 1
    )
    unit = unit.astype(BF)
    turned = [dot_tn(ref[...], unit).astype(BF) for ref in (attn_ref, out_ref)]
    parts = [qkv_ref[0], qkv_ref[1], kv_ref[0], kv_ref[1], q_ref[...]] + turned
    for i, part in enumerate(parts):
        w_ref[:, i * wide : (i + 1) * wide] = part


def pack_weights(w_qkv, w_cross_kv, w_cross_q, w_attn_out, w_cross_out):
    rows, wide = w_cross_q.shape
    whole = pl.BlockSpec(memory_space=pltpu.VMEM)
    return pl.pallas_call(
        pack_weights_body,
        in_specs=[whole] * 5,
        out_specs=whole,
        out_shape=jax.ShapeDtypeStruct((rows, 7 * wide), BF),
        compiler_params=pltpu.CompilerParams(vmem_limit_bytes=8 << 20),
        name="pack_weights",
    )(w_qkv, w_cross_kv, w_cross_q, w_attn_out, w_cross_out)


def mix_body(blocks, mix_ref, bank_ref, mod2_ref, kern_ref, sums_ref):
    count = kern_ref.shape[0]
    wide = kern_ref.shape[3]

    @pl.when(pl.program_id(0) == 0)
    def _():
        sums_ref[...] = jnp.zeros_like(sums_ref)

    total = jnp.zeros((count, wide), F32)
    for block in range(blocks):
        rows = slice(block * CH, (block + 1) * CH)
        part = bank_ref[:, 0, rows, :].reshape(-1, wide)
        low = jnp.dot(mix_ref[...], part, preferred_element_type=F32).astype(BF)
        kern_ref[:, 0, rows, :] = low.reshape(count, CH, wide)
        full = low.astype(F32)
        square = full * full * mod2_ref[block]
        total = total + jnp.sum(square.reshape(count, CH, wide), axis=1)
    sums_ref[...] += total


def mix_kernels(mix_wide, bank, mod2_cols):
    kinds, taps, deep, wide = bank.shape
    count = mix_wide.shape[0] // CH
    return pl.pallas_call(
        partial(mix_body, deep // CH),
        grid=(taps,),
        in_specs=[
            pl.BlockSpec(mix_wide.shape, lambda t: (0, 0)),
            pl.BlockSpec((kinds, 1, deep, wide), lambda t: (0, t, 0, 0)),
            pl.BlockSpec(mod2_cols.shape, lambda t: (0, 0, 0)),
        ],
        out_specs=[
            pl.BlockSpec((count, 1, deep, wide), lambda t: (0, t, 0, 0)),
            pl.BlockSpec((count, wide), lambda t: (0, 0)),
        ],
        out_shape=[
            jax.ShapeDtypeStruct((count, taps, deep, wide), BF),
            jax.ShapeDtypeStruct((count, wide), F32),
        ],
        compiler_params=pltpu.CompilerParams(vmem_limit_bytes=16 << 20),
        name="mix_kernels",
    )(mix_wide, in_hbm(bank), mod2_cols)


def select_windows():
    out = np.zeros((3, HALF + 2, RES, HALF, HALF), np.float32)
    for b in range(3):
        for x in range(RES):
            if 0 <= x + b - 1 < RES:
                for y in range(HALF):
                    out[b, y + 1, x, y, (x + b - 1) // 2] = 1.0
    return out.reshape(3 * (HALF + 2) * RES, LOW)


def load_image(head, refs, at, out_ref):
    rows = refs[0].shape[1]
    for k, ref in enumerate(refs):
        place = pl.multiple_of((head ^ k) * rows, rows)
        out_ref[pl.ds(place, rows), :] = ref[at]


def conv_body(per, head_ref, p0, p1, p2, p3, mod_ref, sel_ref, kern_ref, sums_ref, out_ref, image_ref):
    deep, wide = kern_ref.shape[2], kern_ref.shape[3]
    for at in range(per):
        load_image(head_ref[0], (p0, p1, p2, p3), at, image_ref.at[at])
        low = (image_ref[at].astype(F32) * mod_ref[at]).astype(BF)
        wins = jnp.dot(sel_ref[...], low, preferred_element_type=F32).astype(BF)

        def window(tap):
            row_off, col_off = tap // 3, tap % 3
            starts = [
                (col_off * (HALF + 2) + (y + row_off - 1) // 2 + 1) * RES for y in range(RES)
            ]
            return jnp.concatenate([wins[i : i + RES] for i in starts], axis=0)

        if deep % 128 == 0:
            joined = jnp.concatenate([window(tap) for tap in range(9)], axis=1)
            total = jnp.dot(
                joined, kern_ref[at].reshape(9 * deep, wide), preferred_element_type=F32
            )
        else:
            total = jnp.zeros((PIX, wide), F32)
            for tap in range(9):
                total = total + jnp.dot(window(tap), kern_ref[at, tap], preferred_element_type=F32)
        out_ref[at, :PIX] = total.astype(BF)
        high = sums_ref[at].astype(BF).astype(F32)
        rest = sums_ref[at] - high
        row = lax.broadcasted_iota(jnp.int32, (EXTRA, wide), 0)
        out_ref[at, PIX:] = jnp.where(row == 0, high, jnp.where(row == 1, rest, 0.0)).astype(BF)


def conv_forward(head, pieces, modulate, kernels, sums):
    count, taps, deep, wide = kernels.shape
    per = 2
    rows = pieces[0].shape[1]
    select = jnp.asarray(select_windows(), BF)
    return pl.pallas_call(
        partial(conv_body, per),
        grid_spec=pltpu.PrefetchScalarGridSpec(
            num_scalar_prefetch=1,
            grid=(count // per,),
            in_specs=[pl.BlockSpec((per, rows, deep), lambda s, h: (s, 0, 0))] * 4
            + [
                pl.BlockSpec((per, 1, deep), lambda s, h: (s, 0, 0)),
                pl.BlockSpec(select.shape, lambda s, h: (0, 0)),
                pl.BlockSpec((per, taps, deep, wide), lambda s, h: (s, 0, 0, 0)),
                pl.BlockSpec((per, 1, wide), lambda s, h: (s, 0, 0)),
            ],
            out_specs=pl.BlockSpec((per, PIX + EXTRA, wide), lambda s, h: (s, 0, 0)),
            scratch_shapes=[pltpu.VMEM((per, LOW, deep), BF)],
        ),
        out_shape=jax.ShapeDtypeStruct((count, PIX + EXTRA, wide), BF),
        compiler_params=pltpu.CompilerParams(vmem_limit_bytes=16 << 20),
        name="conv_forward",
    )(head, *pieces, modulate[:, None, :], select, kernels, sums[:, None, :])


def conv_back_body(
    per, order_ref, g0, g1, kern_ref, p0, p1, p2, p3, mod2_ref, mod_ref,
    dkern_ref, dgrid_ref, dmod_ref, image_ref,
):
    deep, wide = kern_ref.shape[2], kern_ref.shape[3]
    head = order_ref[order_ref.shape[0] - 1]
    for at in range(per):
        dconv_ref = (g0, g1)[at]
        load_image(head, (p0, p1, p2, p3), at, image_ref.at[at])
        feat = image_ref[at].astype(F32)
        image = (feat * mod_ref[at]).astype(BF).astype(F32)
        turned = jnp.concatenate([image, image], axis=0).T.astype(BF)
        grads = dconv_ref[0, 0, :PIX].astype(F32).reshape(RES, 2, HALF, wide)
        dsq = jnp.sum(dconv_ref[0, 0, PIX:].astype(F32), axis=0, keepdims=True)
        even, odd = grads[:, 0], grads[:, 1]
        none = jnp.zeros((RES, 1, wide), F32)
        after_even = jnp.concatenate([even[:, 1:], none], axis=1)
        before_odd = jnp.concatenate([none, odd[:, :-1]], axis=1)
        by_col = (odd + after_even, even + odd, before_odd + even)
        gap = jnp.zeros((1, HALF, wide), F32)
        into = jnp.zeros((2 * LOW, deep), F32)
        squares = jnp.zeros((deep, wide), F32)
        scaled = 2.0 * mod2_ref[at] * dsq
        for col_off in range(3):
            rows = by_col[col_off].reshape(HALF, 2, HALF, wide)
            first, second = rows[:, 0], rows[:, 1]
            by_row = (
                second + jnp.concatenate([first[1:], gap], axis=0),
                first + second,
                jnp.concatenate([gap, second[:-1]], axis=0) + first,
            )
            for row_off in range(3):
                tap = 3 * row_off + col_off
                exact = by_row[row_off].reshape(LOW, wide)
                high = exact.astype(BF)
                rest = (exact - high.astype(F32)).astype(BF)
                both = jnp.concatenate([high, rest], axis=0)
                kern = kern_ref[at, tap]
                full = kern.astype(F32)
                grad = jnp.dot(turned, both, preferred_element_type=F32)
                dkern_ref[at, tap] = (grad + full * scaled).astype(BF)
                squares = squares + full * full
                into = into + lax.dot_general(
                    both, kern, (((1,), (1,)), ((), ())), preferred_element_type=F32
                )
        dlow = into[:LOW] + into[LOW:]
        dgrid_ref[at] = dlow * mod_ref[at]
        direct = jnp.sum(dlow * feat, axis=0, keepdims=True)
        through = lax.dot_general(
            jnp.broadcast_to(dsq, (8, wide)),
            squares,
            (((1,), (1,)), ((), ())),
            precision=HIGH,
            preferred_element_type=F32,
        )
        dmod_ref[at] = direct + 2.0 * mod_ref[at] * through[:1]


def conv_backward(order, dconv, kernels, pieces, mod2_col, modulate):
    count, taps, deep, wide = kernels.shape
    slots = dconv.shape[1]
    per = 2
    rows = pieces[0].shape[1]

    def grads_of(at):
        return pl.BlockSpec(
            (1, 1, PIX + EXTRA, wide),
            lambda s, o: (o[(s * per + at) // slots], (s * per + at) % slots, 0, 0),
        )

    grid_spec = pltpu.PrefetchScalarGridSpec(
        num_scalar_prefetch=1,
        grid=(count // per,),
        in_specs=[grads_of(0), grads_of(1)]
        + [pl.BlockSpec((per, taps, deep, wide), lambda s, o: (s, 0, 0, 0))]
        + [pl.BlockSpec((per, rows, deep), lambda s, o: (s, 0, 0))] * 4
        + [
            pl.BlockSpec((per, deep, 1), lambda s, o: (s, 0, 0)),
            pl.BlockSpec((per, 1, deep), lambda s, o: (s, 0, 0)),
        ],
        out_specs=[
            pl.BlockSpec((per, taps, deep, wide), lambda s, o: (s, 0, 0, 0)),
            pl.BlockSpec((per, LOW, deep), lambda s, o: (s, 0, 0)),
            pl.BlockSpec((per, 1, deep), lambda s, o: (s, 0, 0)),
        ],
        scratch_shapes=[pltpu.VMEM((per, LOW, deep), BF)],
    )
    return pl.pallas_call(
        partial(conv_back_body, per),
        grid_spec=grid_spec,
        out_shape=[
            jax.ShapeDtypeStruct((count, taps, deep, wide), BF),
            jax.ShapeDtypeStruct((count, LOW, deep), F32),
            jax.ShapeDtypeStruct((count, 1, deep), F32),
        ],
        compiler_params=pltpu.CompilerParams(vmem_limit_bytes=24 << 20),
        name="conv_backward",
    )(order, dconv, dconv, kernels, *pieces, mod2_col, modulate)


def bank_back_body(blocks, mix_ref, dkern_ref, bank_ref, gbank_ref, cross_ref):
    wide = bank_ref.shape[3]

    @pl.when(pl.program_id(0) == 0)
    def _():
        cross_ref[...] = jnp.zeros_like(cross_ref)

    total = jnp.zeros(cross_ref.shape, F32)
    for block in range(blocks):
        rows = slice(block * CH, (block + 1) * CH)
        grads = dkern_ref[:, 0, rows, :].reshape(-1, wide)
        part = bank_ref[:, 0, rows, :].reshape(-1, wide)
        out = jnp.dot(mix_ref[...], grads, preferred_element_type=F32)
        gbank_ref[:, 0, rows, :] = out.reshape(-1, CH, wide)
        total = total + lax.dot_general(
            grads, part, (((1,), (1,)), ((), ())), preferred_element_type=F32
        )
    cross_ref[...] += total


def bank_backward(mix_wide_t, dkernels, bank):
    kinds, taps, deep, wide = bank.shape
    count = dkernels.shape[0]
    return pl.pallas_call(
        partial(bank_back_body, deep // CH),
        grid=(taps,),
        in_specs=[
            pl.BlockSpec(mix_wide_t.shape, lambda t: (0, 0)),
            pl.BlockSpec((count, 1, deep, wide), lambda t: (0, t, 0, 0)),
            pl.BlockSpec((kinds, 1, deep, wide), lambda t: (0, t, 0, 0)),
        ],
        out_specs=[
            pl.BlockSpec((kinds, 1, deep, wide), lambda t: (0, t, 0, 0)),
            pl.BlockSpec((count * CH, kinds * CH), lambda t: (0, 0)),
        ],
        out_shape=[
            jax.ShapeDtypeStruct(bank.shape, F32),
            jax.ShapeDtypeStruct((count * CH, kinds * CH), F32),
        ],
        compiler_params=pltpu.CompilerParams(vmem_limit_bytes=16 << 20),
        name="bank_backward",
    )(mix_wide_t, dkernels, in_hbm(bank))


NT = (((1,), (1,)), ((), ()))
TN = (((0,), (0,)), ((), ()))


def full(x):
    zeros = (0,) * len(x.shape)
    return pl.BlockSpec(x.shape, lambda i: zeros, pipeline_mode=pl.Buffered(1))


def call_whole(body, scalars, operands, outs, scratch, limit, name):
    operands = [in_hbm(x) for x in operands]
    return pl.pallas_call(
        body,
        grid=(1,),
        in_specs=[pl.BlockSpec(memory_space=pltpu.SMEM)] * len(scalars) + [full(x) for x in operands],
        out_specs=[full(x) for x in outs],
        out_shape=outs,
        scratch_shapes=scratch,
        compiler_params=pltpu.CompilerParams(vmem_limit_bytes=limit << 20),
        name=name,
    )(*scalars, *operands)


def dot_nt(a, b):
    return lax.dot_general(a, b, NT, preferred_element_type=F32)


def dot_tn(a, b):
    return lax.dot_general(a, b, TN, preferred_element_type=F32)


def dot_nn(a, b):
    return jnp.dot(a, b, preferred_element_type=F32)


def pick(ref, index, size):
    return ref[pl.ds(pl.multiple_of(index * size, size), size), :]


def pick_cols(index, size):
    return pl.ds(pl.multiple_of(index * size, size), size)


def self_probs(q_head, score_scale):
    products = dot_nt(q_head, q_head)
    full = q_head.astype(F32)
    ones = jnp.ones((8, q_head.shape[1]), F32)
    key_square = lax.dot_general(ones, full * full, NT, precision=HIGH, preferred_element_type=F32)[:1]
    scores = (2.0 * products - key_square) * score_scale
    raised = jnp.exp(scores - jnp.max(scores, axis=-1, keepdims=True))
    return raised / jnp.sum(raised, axis=-1, keepdims=True)


def attend_body(score_scale, head_ref, p0, p1, p2, p3, w_ref, q_ref, v_ref, att_ref):
    wide = p0.shape[2]
    total = jnp.zeros((p0.shape[1], 2 * wide), F32)
    for k, piece in enumerate((p0, p1, p2, p3)):
        total = total + dot_nn(piece[0], pick(w_ref, head_ref[0] ^ k, wide))
    low = total.astype(BF)
    queries, values = low[:, :wide], low[:, wide:]
    q_ref[0] = queries
    v_ref[0] = values
    for h in range(wide // DH):
        cols = slice(h * DH, (h + 1) * DH)
        probs = self_probs(queries[:, cols], score_scale).astype(BF)
        out = dot_nn(probs, values[:, cols]).astype(BF)
        att_ref[:, 0, :, cols] = out.reshape(att_ref.shape[0], att_ref.shape[2], DH)


def attend(head, pieces, weights, score_scale):
    slots, pix, wide = pieces[0].shape
    wide_all = weights.shape[0]
    one = pl.BlockSpec((1, pix, wide), lambda s, h: (s, 0, 0))
    return pl.pallas_call(
        partial(attend_body, score_scale),
        grid_spec=pltpu.PrefetchScalarGridSpec(
            num_scalar_prefetch=1,
            grid=(slots,),
            in_specs=[one] * 4 + [pl.BlockSpec((wide_all, 2 * wide), lambda s, h: (0, 0))],
            out_specs=[one] * 2 + [pl.BlockSpec((4, 1, pix // 4, wide), lambda s, h: (0, s, 0, 0))],
        ),
        out_shape=[jax.ShapeDtypeStruct((slots, pix, wide), BF)] * 2
        + [jax.ShapeDtypeStruct((4, slots, pix // 4, wide), BF)],
        compiler_params=pltpu.CompilerParams(vmem_limit_bytes=14 << 20),
        name="attend",
    )(head, *pieces, in_hbm(weights))


def attend_back_body(score_scale, head_ref, q_ref, v_ref, datt_ref, w_ref, dqkv_ref, keep_ref, send_ref):
    wide = q_ref.shape[2]
    queries, values = q_ref[0], v_ref[0]
    datt = datt_ref[:, 0].reshape(queries.shape)
    ones = jnp.ones((q_ref.shape[1], DH), BF)
    for h in range(wide // DH):
        cols = slice(h * DH, (h + 1) * DH)
        q_head, dout = queries[:, cols], datt[:, cols]
        probs = self_probs(q_head, score_scale)
        dprobs = dot_nt(dout, values[:, cols])
        dqkv_ref[0, :, wide + h * DH : wide + (h + 1) * DH] = dot_tn(probs.astype(BF), dout).astype(BF)
        dscores = (probs * (dprobs - jnp.sum(probs * dprobs, axis=-1, keepdims=True))).astype(BF)
        as_query = dot_nn(dscores, q_head)
        keyed = dot_tn(dscores, jnp.concatenate([q_head, ones], axis=1))
        dshared = as_query + keyed[:, :DH] - q_head.astype(F32) * keyed[:, DH:]
        dqkv_ref[0, :, cols] = (dshared * (2.0 * score_scale)).astype(BF)
    grads = dqkv_ref[0]
    for k in range(4):
        out_ref = (keep_ref, send_ref)[k % 2]
        out_ref[k // 2, 0] = dot_nt(grads, pick(w_ref, head_ref[0] ^ k, wide))


def attend_back(head, queries, values, datt, weights, score_scale):
    slots, pix, wide = queries.shape
    wide_all = weights.shape[0]
    one = pl.BlockSpec((1, pix, wide), lambda s, h: (s, 0, 0))
    return pl.pallas_call(
        partial(attend_back_body, score_scale),
        grid_spec=pltpu.PrefetchScalarGridSpec(
            num_scalar_prefetch=1,
            grid=(slots,),
            in_specs=[one] * 2
            + [
                pl.BlockSpec((4, 1, pix // 4, wide), lambda s, h: (0, s, 0, 0)),
                pl.BlockSpec((wide_all, 2 * wide), lambda s, h: (0, 0)),
            ],
            out_specs=[
                pl.BlockSpec((1, pix, 2 * wide), lambda s, h: (s, 0, 0)),
                pl.BlockSpec((2, 1, pix, wide), lambda s, h: (0, s, 0, 0)),
                pl.BlockSpec((2, 1, pix, wide), lambda s, h: (0, s, 0, 0)),
            ],
        ),
        out_shape=[
            jax.ShapeDtypeStruct((slots, pix, 2 * wide), BF),
            jax.ShapeDtypeStruct((2, slots, pix, wide), F32),
            jax.ShapeDtypeStruct((2, slots, pix, wide), F32),
        ],
        compiler_params=pltpu.CompilerParams(vmem_limit_bytes=16 << 20),
        name="attend_back",
    )(head, queries, values, datt, in_hbm(weights))


def own_heads_only(tokens, n_tok):
    wide = tokens.shape[1]
    n_head = wide // DH
    tiled = jnp.concatenate([tokens] * n_head, axis=0)
    row = lax.broadcasted_iota(jnp.int32, tiled.shape, 0) // n_tok
    col = lax.broadcasted_iota(jnp.int32, tiled.shape, 1) // DH
    return jnp.where(row == col, tiled, jnp.zeros_like(tiled))


def cross_probs(keys, queries, n_tok, score_scale):
    scores = dot_nt(keys, queries) * score_scale
    shaped = scores.reshape(-1, n_tok, scores.shape[1])
    raised = jnp.exp(shaped - jnp.max(shaped, axis=1, keepdims=True))
    return (raised / jnp.sum(raised, axis=1, keepdims=True)).reshape(scores.shape)


def cross_body(
    slots, n_tok, score_scale, head_ref, att_ref, s0, s1, s2, s3, w0, w1, w2, w3, k0, k1, k2, k3,
    low1_ref, stream2_ref, low2_ref, cq_ref, cout_ref,
):
    weights, kvs = (w0, w1, w2, w3), (k0, k1, k2, k3)
    wide = cq_ref.shape[2]
    rows = att_ref.shape[1] // slots
    for k, piece in enumerate((s0, s1, s2, s3)):
        stream2_ref[:, pick_cols(head_ref[0] ^ k, wide)] = piece[...]
    stream = stream2_ref[...]
    for k in range(4):
        stream = stream + dot_nt(att_ref[head_ref[0] ^ k], weights[k][:, wide : 2 * wide])
    low1 = stream.astype(BF)
    low1_ref[...] = low1
    stream2_ref[...] = stream
    for k in range(4):
        queries = dot_nn(low1, weights[k][:, :wide]).astype(BF)
        cq_ref[k] = queries
        couts = []
        for s in range(slots):
            here = slice(s * rows, (s + 1) * rows)
            kv = kvs[k][s * n_tok : (s + 1) * n_tok, :]
            keys = own_heads_only(kv[:, :wide], n_tok)
            probs = cross_probs(keys, queries[here], n_tok, score_scale).astype(BF)
            couts.append(dot_tn(probs, own_heads_only(kv[:, wide:], n_tok)).astype(BF))
        cout_ref[k] = jnp.concatenate(couts, axis=0)
    stream = stream2_ref[...]
    for k in range(4):
        stream = stream + dot_nt(cout_ref[k], weights[k][:, 2 * wide :])
    stream2_ref[...] = stream
    low2_ref[...] = stream.astype(BF)


def cross_forward(head, att_pix, stream0, weights, kvs, slots, n_tok, score_scale):
    rows, wide = stream0[0].shape
    wide_all = 4 * wide
    outs = [
        jax.ShapeDtypeStruct((rows, wide_all), BF),
        jax.ShapeDtypeStruct((rows, wide_all), F32),
        jax.ShapeDtypeStruct((rows, wide_all), BF),
        jax.ShapeDtypeStruct((4, rows, wide), BF),
        jax.ShapeDtypeStruct((4, rows, wide), BF),
    ]
    body = partial(cross_body, slots, n_tok, score_scale)
    operands = [att_pix, *stream0, *weights, *kvs]
    return call_whole(body, [head], operands, outs, [], 22, "cross_forward")


def cross_back_body(
    slots, n_tok, score_scale, head_ref, dstream_ref, w0, w1, w2, w3, k0, k1, k2, k3, cq_ref, cout_ref,
    low1_ref, trio_ref, dcols_ref, datt_ref, swap_ref, keep_ref, send_ref,
):
    weights, kvs = (w0, w1, w2, w3), (k0, k1, k2, k3)
    wide = cq_ref.shape[2]
    rows = dstream_ref.shape[0] // slots
    n_head = wide // DH
    dstream = dstream_ref[...]
    dcross = dstream.astype(BF)
    trio_ref[0] = low1_ref[...]
    trio_ref[1] = dcross
    row = lax.broadcasted_iota(jnp.int32, (n_head * n_tok, wide), 0) // n_tok
    col = lax.broadcasted_iota(jnp.int32, (n_head * n_tok, wide), 1) // DH
    own = row == col

    def fold(x):
        return jnp.sum(jnp.where(own, x, 0.0).reshape(n_head, n_tok, wide), axis=0)

    for k in range(4):
        owner = head_ref[0] ^ k
        dcout = dot_nn(dcross, weights[k][:, 2 * wide :]).astype(BF)
        dcqs = []
        for s in range(slots):
            here = slice(s * rows, (s + 1) * rows)
            toks = slice(s * n_tok, (s + 1) * n_tok)
            kv = kvs[k][toks, :]
            keys = own_heads_only(kv[:, :wide], n_tok)
            queries = cq_ref[k, here]
            probs = cross_probs(keys, queries, n_tok, score_scale)
            dprobs = dot_nt(own_heads_only(kv[:, wide:], n_tok), dcout[here])
            both = (probs * dprobs).reshape(n_head, n_tok, rows)
            inner = jnp.broadcast_to(jnp.sum(both, axis=1, keepdims=True), both.shape)
            dscores = (probs * (dprobs - inner.reshape(probs.shape))).astype(BF)
            dcqs.append((dot_tn(dscores, keys) * score_scale).astype(BF))
            out_ref = (keep_ref, send_ref)[k % 2]
            out_ref[k // 2, toks, :wide] = fold(dot_nn(dscores, queries)) * score_scale
            out_ref[k // 2, toks, wide:] = fold(dot_nn(probs.astype(BF), dcout[here]))
        dcq = jnp.concatenate(dcqs, axis=0)
        swap_ref[k] = jnp.concatenate([dcq, cout_ref[k]], axis=1)
    for k in range(4):
        dcq = swap_ref[k, :, :wide]
        dstream = dstream + dot_nt(dcq, weights[k][:, :wide])
    dattn = dstream.astype(BF)
    trio_ref[2] = dattn
    for k in range(4):
        dcols_ref[k] = dattn[:, k * wide : (k + 1) * wide]
        datt_ref[head_ref[0] ^ k] = dot_nn(dattn, weights[k][:, wide : 2 * wide]).astype(BF)


def cross_back(head, dstream, weights, kvs, cq, cout, low1, slots, n_tok, score_scale):
    rows, wide_all = dstream.shape
    wide = cq.shape[2]
    outs = [
        jax.ShapeDtypeStruct((3, rows, wide_all), BF),
        jax.ShapeDtypeStruct((4, rows, wide), BF),
        jax.ShapeDtypeStruct((4, rows, wide), BF),
        jax.ShapeDtypeStruct((4, rows, 2 * wide), BF),
        jax.ShapeDtypeStruct((2, slots * n_tok, 2 * wide), F32),
        jax.ShapeDtypeStruct((2, slots * n_tok, 2 * wide), F32),
    ]
    body = partial(cross_back_body, slots, n_tok, score_scale)
    operands = [dstream, *weights, *kvs, cq, cout, low1]
    return call_whole(body, [head], operands, outs, [], 22, "cross_back")


GELU_A = 0.7978845608028654
GELU_B = 0.044715


def mlp_body(
    x0, x1, x2, x3, d0, d1, d2, d3, w_ref,
    dkeep_ref, dsend_ref, fkeep_ref, fsend_ref, active_ref, dhidden_ref, full_ref, dfull_ref,
):
    rows = x0.shape[0]
    hidden_own = w_ref.shape[2]
    chunk = min(512, hidden_own)
    for k, (x, d) in enumerate(zip((x0, x1, x2, x3), (d0, d1, d2, d3))):
        full_ref[k * rows : (k + 1) * rows] = x[...]
        dfull_ref[k * rows : (k + 1) * rows] = d[...]
    for at in range(0, hidden_own, chunk):
        cols = slice(at, at + chunk)
        hidden = dot_nn(full_ref[...], w_ref[0, :, cols])
        square = hidden * hidden
        bent = jnp.tanh(GELU_A * hidden * (1.0 + GELU_B * square))
        active_ref[:, cols] = (0.5 * hidden * (1.0 + bent)).astype(BF)
        slope = 0.5 * (1.0 + bent) + 0.5 * hidden * (1.0 - bent * bent) * GELU_A * (
            1.0 + 3.0 * GELU_B * square
        )
        dactive = dot_nn(dfull_ref[...], w_ref[1, :, cols])
        dhidden_ref[:, cols] = (slope * dactive).astype(BF)
    for k in range(4):
        here = slice(k * rows, (k + 1) * rows)
        (dkeep_ref, dsend_ref)[k % 2][k // 2] = dot_nt(dhidden_ref[here], w_ref[0])
        (fkeep_ref, fsend_ref)[k % 2][k // 2] = dot_nt(active_ref[here], w_ref[1]).astype(BF)


def mlp_both(xs, ds, weights):
    rows, wide_all = xs[0].shape
    hidden = weights.shape[2]
    outs = [jax.ShapeDtypeStruct((2, rows, wide_all), F32)] * 2
    outs += [jax.ShapeDtypeStruct((2, rows, wide_all), BF)] * 2
    outs += [jax.ShapeDtypeStruct((4 * rows, hidden), BF)] * 2
    scratch = [pltpu.VMEM((4 * rows, wide_all), BF)] * 2
    return call_whole(mlp_body, [], [*xs, *ds, weights], outs, scratch, 28, "mlp_both")


def activation(raw, demod, vecs, noise):
    return raw * demod + vecs[0:1] * noise + vecs[1:2]


def conv_post_body(head_ref, got_ref, vecs_ref, noise_ref, raw_ref, demod_ref, cols_ref, blocks_ref, stream_ref):
    total = got_ref[0, 0].astype(F32)
    for m in range(1, got_ref.shape[0]):
        total = total + got_ref[m, 0].astype(F32)
    raw = total[:PIX]
    demod = lax.rsqrt(total[PIX : PIX + 1] + total[PIX + 1 : PIX + 2] + DEMOD_EPS)
    value = activation(raw, demod, vecs_ref[...], noise_ref[0])
    value = jnp.where(value > 0, value, SLOPE * value) * ROOT_TWO
    raw_ref[0] = raw
    demod_ref[0] = demod
    cols_ref[0] = value.astype(BF)
    stream_ref[...] = value
    rows = blocks_ref.shape[2]
    for k in range(4):
        blocks_ref[k, 0] = pick(stream_ref, head_ref[0] ^ k, rows)


def conv_post(head, got, vecs, noise, own_pix):
    n_dp, slots, rows, wide = got.shape
    one = pl.BlockSpec((1, PIX, wide), lambda s, h: (s, 0, 0))
    return pl.pallas_call(
        conv_post_body,
        grid_spec=pltpu.PrefetchScalarGridSpec(
            num_scalar_prefetch=1,
            grid=(slots,),
            in_specs=[
                pl.BlockSpec((n_dp, 1, rows, wide), lambda s, h: (0, s, 0, 0)),
                pl.BlockSpec((2, wide), lambda s, h: (0, 0)),
                pl.BlockSpec((1, PIX, 1), lambda s, h: (s, 0, 0)),
            ],
            out_specs=[
                one,
                pl.BlockSpec((1, 1, wide), lambda s, h: (s, 0, 0)),
                one,
                pl.BlockSpec((4, 1, own_pix, wide), lambda s, h: (0, s, 0, 0)),
            ],
            scratch_shapes=[pltpu.VMEM((PIX, wide), F32)],
        ),
        out_shape=[
            jax.ShapeDtypeStruct((slots, PIX, wide), F32),
            jax.ShapeDtypeStruct((slots, 1, wide), F32),
            jax.ShapeDtypeStruct((slots, PIX, wide), BF),
            jax.ShapeDtypeStruct((4, slots, own_pix, wide), F32),
        ],
        compiler_params=pltpu.CompilerParams(vmem_limit_bytes=(8 << 20) + 4 * n_dp * rows * wide),
        name="conv_post",
    )(head, got, vecs, noise)


def back_post_body(
    keep_ref, got_ref, other_ref, dcols_ref, raw_ref, demod_ref, vecs_ref, noise_ref, dconv_ref, part_ref, work_ref
):
    wide = raw_ref.shape[2]
    dout = keep_ref[0, 0] + got_ref[0, 0] + other_ref[0].astype(F32)
    dout = dout + dcols_ref[:, 0].astype(F32).reshape(PIX, wide)
    raw, demod, noise = raw_ref[0], demod_ref[0], noise_ref[0]
    value = activation(raw, demod, vecs_ref[...], noise)
    dpre = dout * ROOT_TWO * jnp.where(value > 0, 1.0, SLOPE)
    part_ref[0, 0:1] = jnp.sum(dpre * noise, axis=0, keepdims=True)
    part_ref[0, 1:2] = jnp.sum(dpre, axis=0, keepdims=True)
    dsq = jnp.sum(dpre * raw, axis=0, keepdims=True) * -0.5 * demod * demod * demod
    scaled = dpre * demod
    for at in range(wide // 128):
        cols = slice(at * 128, (at + 1) * 128)
        work_ref[at] = scaled[:, cols]
        for y in range(RES):
            both = [work_ref[at, pl.ds(RES * y + par, HALF, stride=2), :] for par in range(2)]
            dconv_ref[0, RES * y : RES * (y + 1), cols] = jnp.concatenate(both, axis=0).astype(BF)
    high = dsq.astype(BF).astype(F32)
    row = lax.broadcasted_iota(jnp.int32, (EXTRA, wide), 0)
    dconv_ref[0, PIX:] = jnp.where(row == 0, high, jnp.where(row == 1, dsq - high, 0.0)).astype(BF)


def back_post(keep, got, other, dcols, raw, demod, vecs, noise):
    slots, pix, wide = raw.shape
    own_pix = dcols.shape[2]
    first = pl.BlockSpec((1, 1, pix, wide), lambda s: (0, s, 0, 0))
    one = pl.BlockSpec((1, pix, wide), lambda s: (s, 0, 0))
    return pl.pallas_call(
        back_post_body,
        grid=(slots,),
        in_specs=[
            first,
            first,
            one,
            pl.BlockSpec((4, 1, own_pix, wide), lambda s: (0, s, 0, 0)),
            one,
            pl.BlockSpec((1, 1, wide), lambda s: (s, 0, 0)),
            pl.BlockSpec((2, wide), lambda s: (0, 0)),
            pl.BlockSpec((1, pix, 1), lambda s: (s, 0, 0)),
        ],
        out_specs=[
            pl.BlockSpec((1, pix + EXTRA, wide), lambda s: (s, 0, 0)),
            pl.BlockSpec((1, 2, wide), lambda s: (s, 0, 0)),
        ],
        out_shape=[
            jax.ShapeDtypeStruct((slots, pix + EXTRA, wide), BF),
            jax.ShapeDtypeStruct((slots, 2, wide), F32),
        ],
        scratch_shapes=[pltpu.VMEM((wide // 128, pix, 128), F32)],
        compiler_params=pltpu.CompilerParams(vmem_limit_bytes=10 << 20),
        name="back_post",
    )(keep, got, other, dcols, raw, demod, vecs, noise)


def store_slots(rank_ref, value, work_ref, keep_ref, send_ref, cols):
    work = work_ref.at[:, : value.shape[1]]
    work[...] = value.astype(BF)
    half = keep_ref.shape[0]
    for m in range(2 * half):
        out_ref = (keep_ref, send_ref)[m // half]
        out_ref[m % half, :, cols] = pick(work, rank_ref[m], BLOCK)


def mlp_grads_body(
    rank_ref, x0, x1, x2, x3, d0, d1, d2, d3, active_ref, dhidden_ref, keep_ref, send_ref, work_ref
):
    hidden = active_ref.shape[1]
    chunk = work_ref.shape[1]
    full = jnp.concatenate([x[...] for x in (x0, x1, x2, x3)], axis=0)
    dfull = jnp.concatenate([d[...] for d in (d0, d1, d2, d3)], axis=0)
    for at in range(0, hidden, chunk):
        cols = slice(at, at + chunk)
        store_slots(rank_ref, dot_tn(full, dhidden_ref[:, cols]), work_ref, keep_ref, send_ref, cols)
        out_cols = slice(hidden + at, hidden + at + chunk)
        store_slots(
            rank_ref, dot_tn(dfull, active_ref[:, cols]), work_ref, keep_ref, send_ref, out_cols
        )


def mlp_grads(rank_of, xs, ds, active, dhidden):
    wide_all, hidden = xs[0].shape[1], active.shape[1]
    outs = [jax.ShapeDtypeStruct((wide_all // BLOCK // 2, BLOCK, 2 * hidden), BF)] * 2
    scratch = [pltpu.VMEM((wide_all, min(512, hidden)), BF)]
    operands = [*xs, *ds, active, dhidden]
    return call_whole(mlp_grads_body, [rank_of], operands, outs, scratch, 24, "mlp_grads")


def mid_grads_body(
    head_ref, rank_ref, t0, t1, t2, t3, s0, s1, s2, s3, att_ref, tok_ref, dkv_ref, keep_ref, send_ref, work_ref
):
    wide = att_ref.shape[2]
    trios = (t0, t1, t2, t3)
    swaps = [s0[...], s1[...], s2[...], s3[...]]
    right = (
        jnp.concatenate([x[:, :wide] for x in swaps], axis=0),
        jnp.concatenate([x[:, wide:] for x in swaps], axis=0),
        jnp.concatenate([att_ref[head_ref[0] ^ k] for k in range(4)], axis=0),
    )
    for i in range(3):
        left = jnp.concatenate([t[i] for t in trios], axis=0)
        cols = slice(i * wide, (i + 1) * wide)
        store_slots(rank_ref, dot_tn(left, right[i]), work_ref, keep_ref, send_ref, cols)
    cols = slice(3 * wide, 5 * wide)
    store_slots(rank_ref, dot_tn(tok_ref[...], dkv_ref[...]), work_ref, keep_ref, send_ref, cols)


def mid_grads(head, rank_of, trios, swapped, attended, tokens, dkv):
    wide_all, wide = trios[0].shape[2], attended.shape[2]
    outs = [jax.ShapeDtypeStruct((wide_all // BLOCK // 2, BLOCK, 5 * wide), BF)] * 2
    scratch = [pltpu.VMEM((wide_all, 2 * wide), BF)]
    operands = [*trios, *swapped, attended, tokens, dkv]
    return call_whole(mid_grads_body, [head, rank_of], operands, outs, scratch, 24, "mid_grads")


def qkv_grads_body(head_ref, rank_ref, p0, p1, p2, p3, dqkv_ref, keep_ref, send_ref, work_ref):
    wide = p0.shape[1]
    for k, piece in enumerate((p0, p1, p2, p3)):
        start = pl.multiple_of((head_ref[0] ^ k) * wide, wide)
        work_ref[pl.ds(start, wide), :] = dot_tn(piece[...], dqkv_ref[...]).astype(BF)
    half = keep_ref.shape[0]
    for m in range(2 * half):
        (keep_ref, send_ref)[m // half][m % half] = pick(work_ref, rank_ref[m], BLOCK)


def qkv_grads(head, rank_of, pieces, dqkv):
    wide = pieces[0].shape[1]
    outs = [jax.ShapeDtypeStruct((4 * wide // BLOCK // 2, BLOCK, dqkv.shape[1]), BF)] * 2
    scratch = [pltpu.VMEM((4 * wide, dqkv.shape[1]), BF)]
    operands = [*pieces, dqkv]
    return call_whole(qkv_grads_body, [head, rank_of], operands, outs, scratch, 14, "qkv_grads")


PLANES = [[0, 2, 4, 6], [1, 3, 5, 7]]


def after(x, *deps):
    return lax.optimization_barrier((x,) + tuple(jax.tree.leaves(deps)))[0]


class Exchange:
    def __init__(self, n_dp, n_h):
        self.n_dp, self.n_h = n_dp, n_h
        self.dp = lax.axis_index("dp").astype(jnp.int32)
        self.head = lax.axis_index("head").astype(jnp.int32)
        ranks = jnp.arange(n_dp, dtype=jnp.int32)
        if n_dp == 8:
            y = self.dp & 1
            self.slot_of = ((ranks & 1) ^ y) * 4 + (ranks >> 1)
            near = self.dp ^ (2 * jnp.arange(4, dtype=jnp.int32))
            self.block_rank = jnp.concatenate([near, near ^ 1])
            places = 2 * jnp.arange(4, dtype=jnp.int32) + y
            self.block_place = jnp.concatenate([places, places ^ 1])
        else:
            self.slot_of = ranks
            self.block_rank = self.block_place = jnp.arange(8, dtype=jnp.int32)

    def hop_head(self, x, step):
        return lax.ppermute(x, "head", [(i, i ^ step) for i in range(self.n_h)])

    def hop_dp(self, x, step):
        return lax.ppermute(x, "dp", [(i, i ^ step) for i in range(self.n_dp)])

    def gather_head(self, x):
        far = self.hop_head(x, 2)
        near = self.hop_head(x, 1)
        return [x, near, far, self.hop_head(far, 1)]

    def start_reduce(self, keep, send):
        got = self.hop_head(send, 1)
        pair = keep[1].astype(F32) + got[1].astype(F32)
        return got, self.hop_head(pair.astype(BF), 2)

    def reduce_head(self, keep, send):
        got, other = self.start_reduce(keep, send)
        return keep[0].astype(F32) + got[0].astype(F32) + other.astype(F32)

    def pair_sums(self, keep, send):
        if self.n_dp != 8:
            x = jnp.concatenate([keep, send])
            x = x.reshape((self.n_dp, -1) + x.shape[2:])
            return lax.all_to_all(x, "dp", 0, 0, tiled=True), None
        return keep, self.hop_dp(send, 1)

    def own_sum(self, pairs, by_place=False, gate=None):
        keep, got = pairs
        if got is None:
            return jnp.sum(keep.astype(F32), axis=0)
        if by_place:
            low = (keep.astype(F32) + got.astype(F32)).astype(BF)
            low = lax.all_to_all(low, "dp", 0, 0, tiled=True, axis_index_groups=PLANES)
            return jnp.sum(low.astype(F32), axis=0)
        pieces = [keep[k].astype(F32) + got[k].astype(F32) for k in range(4)]
        others = [self.hop_dp(pieces[k].astype(BF), 2 * k) for k in range(1, 4)]
        if gate is not None:
            others = lax.optimization_barrier((others, gate))[0]
        return pieces[0] + sum(x.astype(F32) for x in others)

    def gather_z(self, x):
        if self.n_dp != 8:
            return lax.all_gather(x, "dp", axis=0)
        x = jnp.broadcast_to(x[None], (4,) + x.shape)
        return lax.all_to_all(x, "dp", 0, 0, tiled=True, axis_index_groups=PLANES)

    def gather_y(self, x):
        return jnp.concatenate([x, self.hop_dp(x, 1)]) if self.n_dp == 8 else x


def on_device(
    n_dp,
    n_h,
    features,
    style_code,
    labels,
    counts,
    context,
    noise_map,
    w_select,
    w_mod,
    kernel_bank,
    conv_vecs,
    class_table,
    w_qkv,
    w_attn_out,
    w_cross_q,
    w_cross_kv,
    w_cross_out,
    w_mlp_in,
    w_mlp_out,
    w_rgb,
    cot_feat,
    cot_rgb,
):
    ex = Exchange(n_dp, n_h)
    slots, own_low, wide_all = features.shape
    kinds, taps, deep, wide = kernel_bank.shape
    own_pix = cot_feat.shape[1]
    n_tok = context.shape[1]
    count = n_dp * slots
    style_rows = w_select.shape[0]
    style_width = style_code.shape[1]
    hidden_own = w_mlp_in.shape[1]
    score_scale = DH ** (-0.5)
    heads = range(n_h)
    head = ex.head.reshape(1)

    if n_dp == 8:
        message = pack_first(
            labels,
            style_code,
            w_select,
            conv_vecs,
            w_rgb,
            w_mod,
            features.reshape(slots * own_low, wide_all),
        )
        first = lax.all_to_all(message, "dp", 0, 0, tiled=True)
        mod_cols = first[:, :64].reshape(style_width, deep)
        feats = first[:, 64:96].reshape(count, own_low, deep)
        style_all = first[:, 96:104].reshape(count, style_width)
        select_full = first[:, 104:112, :style_rows].transpose(0, 2, 1).reshape(style_width, kinds)
        vecs_full = first[:, 112:114]
        rgb_full = first[:, 114:117]
        labels_all = first[:, 117, : 2 * slots].reshape(n_dp, 2, slots)
    else:

        def to_all(x):
            flat = x.astype(BF).reshape(-1)
            flat = jnp.pad(flat, (0, -flat.size % deep)).reshape(-1, deep)
            return jnp.broadcast_to(flat[None], (n_dp,) + flat.shape)

        message = [
            to_all(style_code),
            to_all(w_select),
            to_all(conv_vecs),
            to_all(w_rgb),
            to_all(jnp.stack([labels // 256, labels % 256])),
            w_mod.reshape(style_rows, n_dp, deep).transpose(1, 0, 2),
            features.reshape(slots * own_low, n_dp, deep).transpose(1, 0, 2),
        ]
        lengths = [m.shape[1] for m in message]
        first = lax.all_to_all(jnp.concatenate(message, axis=1), "dp", 0, 0, tiled=True)
        pieces, at = [], 0
        for length in lengths:
            pieces.append(first[:, at : at + length])
            at += length

        def from_all(piece, *shape):
            size = 1
            for n in shape:
                size *= n
            return piece.reshape(n_dp, -1)[:, :size].reshape((n_dp,) + shape)

        style_all = from_all(pieces[0], slots, style_width).reshape(count, style_width)
        select_full = from_all(pieces[1], style_rows, kinds).reshape(style_width, kinds)
        vecs_full = from_all(pieces[2], 2, deep)
        rgb_full = from_all(pieces[3], 3, deep)
        labels_all = from_all(pieces[4], 2, slots)
        mod_cols = pieces[5].reshape(style_width, deep)
        feats = pieces[6].reshape(count, own_low, deep)
    vecs_full = vecs_full.transpose(1, 0, 2).reshape(2, wide_all)
    rgb_full = rgb_full.transpose(1, 0, 2).reshape(3, wide_all)
    labels_all = labels_all.astype(jnp.int32)
    labels_all = (labels_all[:, 0] * 256 + labels_all[:, 1]).reshape(count)
    feats = ex.gather_head(feats)

    pack = pack_weights(w_qkv, w_cross_kv, w_cross_q, w_attn_out, w_cross_out)
    pack_all = lax.all_gather(pack, "dp", axis=0, tiled=True)
    mlp_pack = jnp.stack([w_mlp_in, w_mlp_out.T])
    mlp_all = lax.all_gather(mlp_pack, "dp", axis=1, tiled=True)
    qkv_w = pack_all
    cross_kv_w = pack_all[:, 2 * wide : 4 * wide]
    cross_w = ex.gather_head(pack_all[:, 4 * wide :])

    table_rows = class_table.shape[0]
    one_hot = (
        labels_all[:, None] == ex.dp * table_rows + jnp.arange(table_rows, dtype=jnp.int32)[None, :]
    )
    class_part = jnp.dot(one_hot.astype(BF), class_table, preferred_element_type=F32).astype(BF)
    class_got = lax.all_to_all(class_part.reshape(n_dp, slots, wide_all), "dp", 0, 0, tiled=True)
    class_rows = jnp.sum(class_got.astype(F32), axis=0)
    tokens = (context.astype(F32) + class_rows[:, None, :]).astype(BF).reshape(slots * n_tok, wide_all)
    cross_kv_own = dot_nn(tokens, cross_kv_w).astype(BF)
    cross_kvs = ex.gather_head(cross_kv_own)

    live_slots = (jnp.arange(slots, dtype=jnp.int32) < counts[0]).astype(F32)
    factor = live_slots / counts[0].astype(F32)
    dcolour = cot_rgb.astype(F32) * factor[:, None, None]
    dstream = cot_feat.astype(F32) * factor[:, None, None] + jnp.einsum(
        "scp,ci->spi", dcolour, rgb_full.astype(F32), precision=HIGH
    )
    dstream = dstream.reshape(slots * own_pix, wide_all)
    dbranches = ex.gather_head(dstream.astype(BF))

    vecs_own = lax.dynamic_slice_in_dim(vecs_full, ex.head * wide, wide, 1).astype(F32)
    noise_cols = noise_map.astype(F32)[:, :, None]
    mixing = jax.nn.softmax(jnp.dot(style_all, select_full, preferred_element_type=F32), axis=-1)
    mixing_low = mixing.astype(BF)
    unit = jnp.eye(CH, dtype=BF)
    mix_wide = (mixing_low[:, None, :, None] * unit[None, :, None, :]).reshape(count * CH, kinds * CH)
    modulate = 1.0 + jnp.dot(style_all, mod_cols, preferred_element_type=F32)
    mod2 = jnp.square(modulate)
    mod2_cols = mod2.reshape(count, deep // CH, CH).transpose(1, 0, 2).reshape(deep // CH, count * CH, 1)
    kernels, square_part = mix_kernels(mix_wide, kernel_bank, mod2_cols)
    conv_part = conv_forward(head, feats, modulate, kernels, square_part)
    conv_part = after(conv_part, class_got)
    conv_got = lax.all_to_all(
        conv_part.reshape(n_dp, slots, PIX + EXTRA, wide), "dp", 0, 0, tiled=True
    )
    conv_got = after(conv_got, *cross_w, *cross_kvs, *dbranches)
    raw, demod, cols_low, blocks = conv_post(head, conv_got, vecs_own, noise_cols, own_pix)

    cols_pieces = ex.gather_head(cols_low)
    rows = slots * own_pix
    blocks = after(blocks, *cols_pieces).reshape(n_h, rows, wide)
    stream0 = [blocks[0]] + [ex.hop_head(blocks[k], k) for k in range(1, n_h)]
    queries, values, attended = attend(head, cols_pieces, qkv_w, score_scale)
    attended = attended.reshape(n_h, rows, wide)
    att_pix = lax.all_to_all(attended, "head", 0, 0, tiled=True)

    low1, stream2, low2, cq, cout = cross_forward(
        head, att_pix, stream0, cross_w, cross_kvs, slots, n_tok, score_scale
    )

    fulls = ex.gather_head(low2)
    dkeep, dsend, fkeep, fsend, active, dhidden = mlp_both(fulls, dbranches, mlp_all)
    dstream = dstream + ex.reduce_head(dkeep, dsend)
    mlp_keep, mlp_send = mlp_grads(ex.block_rank, fulls, dbranches, active, dhidden)
    dstream = after(dstream, mlp_keep)

    trio, dcols, datt, swap, kv_keep, kv_send = cross_back(
        head, dstream, cross_w, cross_kvs, cq, cout, low1, slots, n_tok, score_scale
    )
    mlp_pairs = ex.pair_sums(mlp_keep, after(mlp_send, datt))
    datt_cols = lax.all_to_all(datt, "head", 0, 0, tiled=True).reshape(n_h, slots, own_pix, wide)
    dcols = lax.all_to_all(dcols, "head", 0, 0, tiled=True).reshape(n_h, slots, own_pix, wide)

    dqkv, back_keep, back_send = attend_back(head, queries, values, datt_cols, qkv_w, score_scale)
    back_got, back_other = ex.start_reduce(back_keep, back_send)
    qkv_keep, qkv_send = qkv_grads(
        head,
        ex.block_place,
        [p.reshape(slots * PIX, wide) for p in cols_pieces],
        dqkv.reshape(slots * PIX, 2 * wide),
    )
    back_other = after(back_other, qkv_keep)

    dconv, vecs_part = back_post(
        back_keep, back_got, back_other, dcols, raw, demod, vecs_own, noise_cols
    )
    dconv_half = ex.gather_z(dconv)
    dconv_all = ex.gather_y(dconv_half)

    fkeep, fsend, trio, swap, kv_keep, kv_send, qkv_send, stream2 = lax.optimization_barrier(
        (fkeep, fsend, trio, swap, kv_keep, kv_send, qkv_send, stream2, dconv)
    )[:8]
    trios = ex.gather_head(trio)
    swapped = [swap[0]] + [ex.hop_head(swap[k], k) for k in range(1, n_h)]
    dkv_own = ex.reduce_head(kv_keep, kv_send).astype(BF)
    stream3 = stream2 + ex.reduce_head(fkeep, fsend)
    qkv_pairs = ex.pair_sums(qkv_keep, qkv_send)

    stream3 = stream3.reshape(slots, own_pix, wide_all)
    features_out = (stream3 * live_slots[:, None, None]).astype(BF)
    final_low = stream3.astype(BF)
    colour = dot32("spi,ci->scp", final_low, rgb_full)
    rgb_out = (colour * live_slots[:, None, None]).astype(BF)
    rgb_part = jnp.einsum("scp,spi->ci", dcolour, final_low.astype(F32), precision=HIGH)

    dtokens_sum = jnp.sum(dot_nt(dkv_own, cross_kv_w).reshape(slots, n_tok, wide_all), axis=1)
    mid_keep, mid_send = mid_grads(
        head, ex.block_rank, trios, swapped, attended, tokens, dkv_own
    )
    dconv_all = after(dconv_all, mid_keep, features_out, rgb_out, rgb_part, dtokens_sum)
    mid_pairs = ex.pair_sums(mid_keep, mid_send)
    dkernels, dgrid, dmod = conv_backward(
        jnp.concatenate([ex.slot_of, head]),
        dconv_all,
        kernels,
        feats,
        mod2[:, :, None],
        modulate[:, None, :],
    )
    grad_bank, cross = bank_backward(mix_wide.T, dkernels, kernel_bank)
    dmixing_part = jnp.einsum("saka->sk", cross.reshape(count, CH, kinds, CH))

    grad_mlp = ex.own_sum(mlp_pairs, gate=cross)
    grad_mlp_in, grad_mlp_out = grad_mlp[:, :hidden_own], grad_mlp[:, hidden_own:].T
    mid = ex.own_sum(lax.optimization_barrier((mid_pairs, dkernels))[0])
    grad_cross_q = mid[:, :wide]
    grad_cross_out = mid[:, wide : 2 * wide].T
    grad_attn_out = mid[:, 2 * wide : 3 * wide].T
    grad_cross_kv = jnp.stack([mid[:, 3 * wide : 4 * wide], mid[:, 4 * wide :]])
    qkv_own_grad = ex.own_sum(lax.optimization_barrier((qkv_pairs, dkernels))[0], by_place=True)
    grad_qkv = jnp.stack([qkv_own_grad[:, :wide], qkv_own_grad[:, wide:]])

    everyone = (n_dp, n_h)
    dmix_high, dmix_low = hi_lo(dmixing_part)

    def rows_of(x):
        flat = x.astype(BF).reshape(-1)
        return jnp.pad(flat, (0, -flat.size % deep)).reshape(-1, deep)

    common = [
        rows_of(dmod),
        rows_of(dmix_high),
        rows_of(dmix_low),
        rows_of(jnp.sum(vecs_part, axis=0)),
        rows_of(dtokens_sum),
    ]
    common_lengths = [c.shape[0] for c in common]
    common = jnp.concatenate(common, axis=0)
    to_grid = dgrid.reshape(n_dp, slots, n_h, own_low, deep).transpose(0, 2, 1, 3, 4)
    to_rgb = jnp.broadcast_to(
        rgb_part.reshape(3, n_dp, deep).transpose(1, 0, 2)[:, None], everyone + (3, deep)
    )
    last = jnp.concatenate(
        [
            to_grid.reshape(everyone + (slots * own_low, deep)).astype(BF),
            to_rgb.astype(BF),
            jnp.broadcast_to(common, everyone + common.shape),
        ],
        axis=2,
    )
    last = last.reshape((n_dp * n_h,) + last.shape[2:])
    last = lax.all_to_all(last, ("dp", "head"), 0, 0, tiled=True)
    last = last.astype(F32).reshape(everyone + last.shape[1:])
    grid_rows = slots * own_low
    grad_input = jnp.sum(last[:, :, :grid_rows], axis=1).reshape(n_dp, slots, own_low, deep)
    grad_input = grad_input.transpose(1, 2, 0, 3).reshape(slots, own_low, wide_all)
    grad_rgb = jnp.sum(last[:, :, grid_rows : grid_rows + 3], axis=(0, 1))
    got, at = [], grid_rows + 3
    for length in common_lengths:
        got.append(last[:, :, at : at + length])
        at += length

    def values_of(piece, size):
        return piece.reshape(piece.shape[:-2] + (-1,))[..., :size]

    dmodulate = values_of(jnp.sum(got[0], axis=1), count * deep).reshape(n_dp, count, deep)
    dmodulate = dmodulate.transpose(1, 0, 2).reshape(count, wide_all)
    dmixing = jnp.sum(got[1] + got[2], axis=(0, 1))
    dmixing = values_of(dmixing, count * kinds).reshape(count, kinds)
    vecs_sum = values_of(jnp.sum(got[3], axis=0), 2 * wide).reshape(n_h, 2, wide)
    vecs_sum = vecs_sum.transpose(1, 0, 2).reshape(2, wide_all)
    grad_vecs = lax.dynamic_slice_in_dim(vecs_sum, ex.dp * deep, deep, 1)
    dtok_all = values_of(jnp.sum(got[4], axis=1), slots * wide_all).reshape(count, wide_all)

    style_own = lax.dynamic_slice_in_dim(style_all, ex.dp * style_rows, style_rows, 1).astype(F32)
    grad_mod = jnp.einsum("sr,sc->rc", style_own, dmodulate, precision=HIGH)
    logit_grad = mixing * (dmixing - jnp.sum(mixing * dmixing, axis=-1, keepdims=True))
    grad_select = jnp.einsum("sr,sk->rk", style_own, logit_grad, precision=HIGH)
    grad_table = jnp.einsum("sr,sc->rc", one_hot.astype(F32), dtok_all, precision=HIGH)

    return (
        features_out,
        rgb_out,
        grad_input,
        grad_select,
        grad_mod,
        grad_bank,
        grad_vecs,
        grad_table,
        grad_qkv,
        grad_attn_out,
        grad_cross_q,
        grad_cross_kv,
        grad_cross_out,
        grad_mlp_in,
        grad_mlp_out,
        grad_rgb,
    )


def solution(mesh):
    return jax.shard_map(
        partial(on_device, mesh.shape["dp"], mesh.shape["head"]),
        mesh=mesh,
        in_specs=(
            P("dp", "head", None),
            P("dp", None),
            P("dp"),
            P("dp"),
            P("dp", None, None),
            P("dp", None),
            P("dp", None),
            P("dp", None),
            P(None, None, "dp", "head"),
            P(None, "dp"),
            P("dp", None),
            P(None, "dp", "head"),
            P("head", "dp"),
            P("dp", "head"),
            P(None, "dp", "head"),
            P("head", "dp"),
            P("dp", "head"),
            P("head", "dp"),
            P(None, "dp"),
            P("dp", "head", None),
            P("dp", None, "head"),
        ),
        out_specs=(
            P("dp", "head", None),
            P("dp", None, "head"),
            P("dp", "head", None),
            P("dp", None),
            P("dp", None),
            P(None, None, "dp", "head"),
            P(None, "dp"),
            P("dp", None),
            P(None, "dp", "head"),
            P("head", "dp"),
            P("dp", "head"),
            P(None, "dp", "head"),
            P("head", "dp"),
            P("dp", "head"),
            P("head", "dp"),
            P(None, "dp"),
        ),
        check_vma=False,
    )
```
